32 devices in a mesh: gx: 8 (over y, x, core), gy: 4 (over z).
Axes of the slice: x: 2, y: 2, z: 4, core: 2. Of those that a mesh axis runs over, the one named last changes fastest.
Arguments:
- velocity: float32 [3, 32, 256, 2048], P(None, None, 'gx', 'gy'), may hold values from -6 to 6
- fiber_points: float32 [256, 3, 128], P(('gx', 'gy')), may hold values from -6 to 6
- stiffness: float32 [256], P(('gx', 'gy')), may hold values from 0.5 to 2
- links: int32 [256, 128], P(('gx', 'gy')), may hold values from 1 to 127
- delta_weights: bfloat16 [256, 8, 128, 512], P(('gx', 'gy')), may hold values from -0.5 to 0.5
- owners: int32 [256, 8, 1], P(('gx', 'gy')), may hold values from 0 to 31; in each aligned block of 64 rows (0 to 63, 64 to 127, ..., all dimensions but the last counted through in order) at most 4 rows name the same one
- patch_slots: int32 [256, 8], P(('gx', 'gy')), may hold values from 0 to 1023
Outputs:
- fluid: float32 [3, 32, 256, 2048], P(None, None, 'gx', 'gy')
- moved_points: float32 [256, 3, 128], P(('gx', 'gy'))
The draws below stay inside these ranges and needn't reach their ends.
Inputs may be any that keep to these rules, and one draw needn't show every extreme that they name: owners counts devices in the order gx slower, gy faster; among the rows of one device, no owner is named more than 4 times, a bound that some block reaches.
All inputs are finite; a program needn't handle non-finite values.
Results may differ from the reference program's by a relative error of at most 0.0037.
Values may be sent and summed in bfloat16 or wider, within the bound.
A program may use at most 128 MiB of HBM per device.

```python
import math
import jax
import jax.numpy as jnp
import numpy as np
from jax import lax

CX = 32
CY = 512
NZ = 32
PATCH = 512
FBP = 128
FBD = 8
INTERSECTION = 8
STEPS = 2
NX = 256
NY = 2048
CAP = 4
P_DEV = 1024
FIBERS_B = 256
N_GX = 8
N_GY = 4
DEVICES = 32


def set_ends(drawn, own_key, smallest, high):
    longest = drawn.shape.index(max(drawn.shape))
    spots = []
    for shift in (0, 1):
        where = [jax.random.randint(jax.random.fold_in(own_key, axis), (), 0, length) for axis, length in enumerate(drawn.shape)]
        where[longest] = (where[longest] + shift) % drawn.shape[longest]
        spots.append(tuple(where))
    return drawn.at[spots[0]].set(smallest).at[spots[1]].set(high)


def steps_of(own_key, shape, split, least, largest):
    gain, own = 1.0, jax.random.fold_in(own_key, 6)
    for axis_at, blocks in split:
        draws = jnp.exp(jax.random.uniform(jax.random.fold_in(own, axis_at), (blocks,), jnp.float32, least / len(split), largest / len(split)))
        gain = gain * jnp.repeat(draws, shape[axis_at] // blocks).reshape([-1 if axis == axis_at else 1 for axis in range(len(shape))])
    return gain


def deal_out(key, own, number, rows, amount, top, most, slope):
    order = jax.random.permutation(key, amount)
    crowded, common = load_shares(amount, rows * top, most, slope, True), load_shares(amount, rows * top, most, slope, False)
    places = jnp.arange(amount)

    def named(lengths, turn):
        used = int((lengths > 0).sum())
        fixed = max(1, used // 4)
        passed = fixed + (places - fixed + turn * (used - fixed)) % max(1, amount - fixed)
        return jnp.zeros((amount,), jnp.int32).at[order[jnp.where(places < fixed, places, passed)]].set(jnp.asarray(lengths, jnp.int32))

    lengths = jnp.where(number % 4 == 0, named(crowded, number // 4), named(common, number - number // 4 - 1))
    mixed = jax.random.permutation(jax.random.fold_in(own, 3), amount)
    donor, taker = mixed[0:amount // 2 * 2:2], mixed[1:amount // 2 * 2:2]
    margin = jnp.minimum(lengths[donor] - 1, most - lengths[taker]) // 2
    margin = jnp.where((donor == order[0]) | (taker == order[0]) | (lengths[taker] == 0), 0, jnp.maximum(margin, 0))
    passed = jax.random.randint(jax.random.fold_in(own, 4), (amount // 2,), 0, 1 << 20) % (margin + 1)
    lengths = lengths.at[donor].add(-passed).at[taker].add(passed)
    labels = jnp.searchsorted(jnp.cumsum(lengths), jnp.arange(rows * top), side="right").astype(jnp.int32)
    grid = labels.reshape(top, rows).T
    grid = grid[jax.random.permutation(jax.random.fold_in(own, 1), rows)]
    turn = jax.random.randint(jax.random.fold_in(own, 2), (rows, 1), 0, top)
    return jnp.take_along_axis(grid, (jnp.arange(top)[None, :] + turn) % top, axis=1)


def load_shares(amount, total, limit, slope, full):
    portions = [(1 << 20) // math.isqrt(rank ** slope) + 1 for rank in range(1, amount + 1)]
    largest = limit if full else min(limit, max(-(-total // amount), total * portions[0] // sum(portions)))
    least = 1 if total - largest >= amount - 1 else 0
    given, surplus = [largest] + [least] * (amount - 1), total - largest - least * (amount - 1)
    while surplus > 0:
        candidates = [i for i in range(1, amount) if given[i] < largest] or [i for i in range(1, amount) if given[i] < limit]
        mass, left = sum([portions[i] for i in candidates]), surplus
        for i in candidates:
            more = min(limit - given[i], max(1, left * portions[i] // mass), surplus)
            given[i] = given[i] + more
            surplus = surplus - more
    return np.array(given)


def bell_draw(stream_key, dims, deviation, bound, shards=(), kind=jnp.bfloat16):
    entries = jax.random.normal(stream_key, dims, jnp.float32) * deviation
    if len(shards) > 0:
        entries = steps_of(stream_key, dims, shards, -0.22, 0.18) * entries
    return jnp.clip(entries, min=-bound, max=bound).astype(kind)


def setup_inputs(seed: int = 0) -> dict:
    seeds = jax.random.split(jax.random.key(seed), 8)
    velocity = bell_draw(seeds[0], (3, NZ, NX, NY), 1.0, 6.0, ((2, 8), (3, 4)), jnp.float32)
    fiber_points = bell_draw(seeds[1], (FIBERS_B, 3, FBP), 1.0, 6.0, ((0, 32),), jnp.float32)
    stiffness = jnp.clip(jnp.exp(math.log(2.0) - 1.3862944 * jax.random.uniform(seeds[2], (FIBERS_B,), jnp.float32) ** steps_of(seeds[2], (FIBERS_B,), ((0, 32),), -0.2, 0.2)), 0.5, 2.0)
    links = set_ends(jax.random.randint(seeds[3], (FIBERS_B, FBP), 1, FBP), jax.random.fold_in(seeds[3], 1), 1, FBP - 1).astype(jnp.int32)
    delta_weights = bell_draw(seeds[4], (FIBERS_B, INTERSECTION, FBP, PATCH), FBP ** -0.5, 0.5, ((0, 32),))
    owners_keys = jax.random.split(jax.random.fold_in(seeds[5], 1), FIBERS_B * INTERSECTION // (FBD * INTERSECTION))
    owners_turns = jax.random.permutation(jax.random.fold_in(seeds[5], 3), FIBERS_B * INTERSECTION // (FBD * INTERSECTION))
    owners = jax.vmap(lambda own, number: deal_out(jax.random.fold_in(seeds[5], 2), own, number, FBD * INTERSECTION, DEVICES, 1, CAP, 2))(owners_keys, owners_turns).reshape((FIBERS_B, INTERSECTION, 1))
    patch_slots = set_ends(jax.random.randint(seeds[6], (FIBERS_B, INTERSECTION), 0, P_DEV), jax.random.fold_in(seeds[6], 1), 0, P_DEV - 1).astype(jnp.int32)
    return dict(velocity=velocity, fiber_points=fiber_points, stiffness=stiffness, links=links, delta_weights=delta_weights, owners=owners, patch_slots=patch_slots)


viscosity = 0.1
transport_rate = 0.1
force_step = 0.5
fiber_step = 0.25


def advance(extended):
    middle = extended[:, :, 1:-1, 1:-1]
    east_cells = extended[:, :, 2:, 1:-1]
    west_cells = extended[:, :, :-2, 1:-1]
    north_cells = extended[:, :, 1:-1, 2:]
    south_cells = extended[:, :, 1:-1, :-2]
    above_cells = jnp.roll(middle, -1, axis=1)
    below_cells = jnp.roll(middle, 1, axis=1)
    laplace = east_cells + west_cells + north_cells + south_cells + above_cells + below_cells - 6.0 * middle
    transport = middle[0:1] * (east_cells - west_cells) + middle[1:2] * (north_cells - south_cells) + middle[2:3] * (above_cells - below_cells)
    return middle + viscosity * laplace - transport_rate * transport


def reference(velocity, fiber_points, stiffness, links, delta_weights, owners, patch_slots):
    device_count = N_GX * N_GY
    patch_count = CX * CY * NZ // PATCH
    partner = (jnp.arange(FBP, dtype=jnp.int32)[None, :] + links) % FBP
    partner_full = jnp.broadcast_to(partner[:, None, :], fiber_points.shape)
    partner_points = jnp.take_along_axis(fiber_points, partner_full, axis=2)
    fiber_force = stiffness[:, None, None] * (partner_points - fiber_points)
    force_bf = fiber_force.astype(jnp.bfloat16)
    contrib = jnp.einsum("bcp,bkpq->bkcq", force_bf.astype(jnp.float32), delta_weights.astype(jnp.float32), precision=lax.Precision.HIGHEST)
    target = (owners[:, :, 0] * patch_count + patch_slots).reshape(-1).astype(jnp.int32)
    patches = jnp.zeros((device_count * patch_count, 3, PATCH), jnp.float32)
    patches = patches.at[target].add(contrib.reshape(-1, 3, PATCH))
    field = patches.reshape(N_GX, N_GY, patch_count, 3, PATCH).transpose(3, 0, 1, 2, 4)
    field = field.reshape(3, N_GX, N_GY, NZ, CX, CY).transpose(0, 3, 1, 4, 2, 5).reshape(3, NZ, NX, NY)
    moving = velocity + force_step * field
    for step_index in range(STEPS):
        moving = advance(jnp.pad(moving, ((0, 0), (0, 0), (1, 1), (1, 1))))
    fluid_bf = moving.astype(jnp.bfloat16)
    patch_view = fluid_bf.reshape(3, NZ, N_GX, CX, N_GY, CY).transpose(2, 4, 0, 1, 3, 5)
    patch_view = patch_view.reshape(device_count, 3, patch_count, PATCH).transpose(0, 2, 1, 3)
    patch_view = patch_view.reshape(device_count * patch_count, 3, PATCH)
    picked = patch_view[target].reshape(FIBERS_B, INTERSECTION, 3, PATCH)
    interp = jnp.einsum("bkcq,bkpq->bcp", picked.astype(jnp.float32), delta_weights.astype(jnp.float32), precision=lax.Precision.HIGHEST)
    return moving, fiber_points + fiber_step * interp
```

```python
import functools

import jax
import jax.numpy as jnp
from jax import lax
from jax.experimental import pallas as pl
from jax.experimental.pallas import tpu as pltpu
from jax.sharding import PartitionSpec as P

STEPS = 2
viscosity = 0.1
transport_rate = 0.1
force_step = 0.5
fiber_step = 0.25

F32 = jnp.float32
BF16 = jnp.bfloat16
I32 = jnp.int32
LANES = 128
MESH = pl.DeviceIdType.MESH
VMEM = pl.BlockSpec(memory_space=pltpu.VMEM)
ANY = pl.BlockSpec(memory_space=pl.ANY)
SMEM = pl.BlockSpec(memory_space=pltpu.SMEM)


def iota(shape, dim):
    return lax.broadcasted_iota(I32, shape, dim)


def to_column(row):
    n = row.shape[1]
    return jnp.sum(jnp.where(iota((n, n), 0) == iota((n, n), 1), row, 0), axis=1, keepdims=True)


def to_row(grid):
    n, k = grid.shape
    tiled = jnp.concatenate([grid] * n, axis=1)
    return jnp.sum(
        jnp.where(iota((n, n * k), 0) == iota((n, n * k), 1) // k, tiled, 0), axis=0, keepdims=True)


def slot_row(owner_row, owner_column, devices):
    n = owner_row.shape[1]
    same = (owner_column == owner_row) & (iota((n, n), 0) < iota((n, n), 1))
    rank = jnp.sum(jnp.where(same, 1, 0), axis=0, keepdims=True)
    return rank * devices + owner_row


def slot_column(owner_row, owner_column, devices):
    n = owner_row.shape[1]
    same = (owner_column == owner_row) & (iota((n, n), 1) < iota((n, n), 0))
    rank = jnp.sum(jnp.where(same, 1, 0), axis=1, keepdims=True)
    return rank * devices + owner_column


def spread(
    devices, per_owner, points_ref, stiffness_ref, links_ref, owners_ref, slots_ref, loaded_ref,
    out_ref, table_ref, contrib_ref, stage_ref, wait_block,
):
    blocks, k, points, patch = loaded_ref.shape
    parts = []
    for c in range(3):
        rest = points_ref[c]
        for _ in range(3):
            part = rest.astype(BF16).astype(F32)
            parts.append(part)
            rest = rest - part
    parts.append(jnp.zeros_like(parts[0]))
    parts = jnp.concatenate(parts, axis=0).astype(BF16)
    partner = lax.rem(iota(links_ref.shape, 1) + links_ref[...], points)
    diagonal = iota((k, k * points), 0) == iota((k, k * points), 1) // points
    lefts = []
    for b in range(blocks):
        moving = one_hot(iota((points, points), 0) == partner[b:b + 1])
        there = jnp.dot(parts, moving, preferred_element_type=F32)
        rows = []
        for c in range(3):
            r = 3 * c * blocks + b
            found = there[r:r + 1] + there[r + blocks:r + blocks + 1]
            found = found + there[r + 2 * blocks:r + 2 * blocks + 1]
            row = stiffness_ref[b] * (found - points_ref[c, b:b + 1, :])
            rows.append(jnp.where(diagonal, jnp.concatenate([row] * k, axis=1), 0.0))
        rows.append(jnp.zeros_like(rows[0]))
        lefts.append(jnp.concatenate(rows, axis=0).astype(BF16))

    owner_row = to_row(owners_ref[:, 0, :])
    places = slot_row(owner_row, to_column(owner_row), devices)
    total = devices * per_owner
    chosen = iota((total, places.shape[1]), 0) == places
    selector = one_hot(chosen)

    for b in range(blocks):
        wait_block(b)
        right = loaded_ref[b].reshape(k * points, patch)
        result = jnp.dot(lefts[b], right, preferred_element_type=F32)
        for c in range(3):
            contrib_ref[c, b * k:(b + 1) * k, :] = result[c * k:(c + 1) * k]

    tiles = patch // LANES
    width = 3 * tiles * per_owner
    for c in range(3):
        packed = jnp.dot(selector, contrib_ref[c].astype(BF16), preferred_element_type=F32)
        for p in range(per_owner):
            for t in range(tiles):
                stage_ref[pl.ds(p * 3 * tiles + c * tiles + t, devices, stride=width), :] = (
                    packed[p * devices:(p + 1) * devices, t * LANES:(t + 1) * LANES]
                )
    out_ref[...] = stage_ref[...].reshape(out_ref.shape).astype(BF16)
    column = jnp.max(jnp.where(chosen, to_row(slots_ref[...]), -1), axis=1, keepdims=True)
    lane = iota((devices, LANES), 1)
    table = jnp.full((devices, LANES), -1, I32)
    for p in range(per_owner):
        table = jnp.where(lane == p, column[p * devices:(p + 1) * devices], table)
    for d in range(devices):
        table_ref[d] = table[d:d + 1]


HBM = pl.BlockSpec(memory_space=pltpu.HBM)


def place(d, columns):
    return (d // columns, lax.rem(d, columns))


def start_swap(columns, devices, ins, outs, send_sem, recv_sem, own_sem):
    count = len(ins)
    me = lax.axis_index("gx") * columns + lax.axis_index("gy")

    def copy(n, off):
        other = lax.rem(me + off, devices)
        return pltpu.make_async_remote_copy(
            src_ref=ins[n].at[other], dst_ref=outs[n].at[me],
            send_sem=send_sem.at[n, off], recv_sem=recv_sem.at[n, off],
            device_id=place(other, columns), device_id_type=MESH,
        )

    def start(off, carry):
        for n in range(count):
            copy(n, off).start()
        return carry

    def finish(off, carry):
        for n in range(count):
            copy(n, off).wait()
        return carry

    def own(n):
        return pltpu.make_async_copy(ins[n].at[me], outs[n].at[me], own_sem.at[n])

    lax.fori_loop(1, devices, start, 0)
    for n in range(count):
        own(n).start()

    def wait():
        for n in range(count):
            own(n).wait()
        lax.fori_loop(1, devices, finish, 0)

    return wait


def swap_sems(count, devices):
    return [
        pltpu.SemaphoreType.DMA((count, devices)),
        pltpu.SemaphoreType.DMA((count, devices)),
        pltpu.SemaphoreType.DMA((count,)),
    ]


def unpack(stage_ref, devices, per_owner, tiles, c):
    width = 3 * tiles * per_owner
    rows = []
    for p in range(per_owner):
        rows.append(jnp.concatenate(
            [stage_ref[pl.ds(p * 3 * tiles + c * tiles + t, devices, stride=width), :]
             for t in range(tiles)], axis=1))
    return jnp.concatenate(rows, axis=0)


def table_row(table_ref, devices, per_owner):
    total = devices * per_owner
    row = jnp.zeros((1, total), I32)
    for p in range(per_owner):
        column = table_ref[:, 0, :][:, p:p + 1]
        spot = iota((devices, total), 1) == p * devices + iota((devices, total), 0)
        row = row + jnp.sum(jnp.where(spot, column, 0), axis=0, keepdims=True)
    return row


def table_column(table_ref, per_owner):
    return jnp.concatenate([table_ref[:, 0, :][:, p:p + 1] for p in range(per_owner)], axis=0)


def one_hot(mask):
    return mask.astype(F32).astype(BF16)


PAD = 8
UNROLL = 4
assert viscosity == transport_rate
keep = 1.0 - 6.0 * viscosity


def sweep(mid, east, west, north, south, above, below):
    coefficients = [(1 - m, 1 + m) for m in mid]
    out = []
    for c in range(3):
        pairs = [
            ahead * front[c] + behind * back[c]
            for (ahead, behind), (front, back) in zip(
                coefficients, ((east, west), (north, south), (above, below)))
        ]
        out.append(pairs[0] + (pairs[1] + pairs[2]))
    return out


def step_kernel(
    rows_grid, columns_grid, per_owner, unroll, points_in, stiffness_in, links_in, owners_in,
    slots_in, weights_ref, velocity_ref,
    fluid_ref, interp_ref, loaded_ref, returned_ref, picked_ref,
    points_ref, stiffness_ref, links_ref, owners_ref, slots_ref, small_sem, received_ref, table_ref, out_ref, outtable_ref, replies_ref, contrib_ref, stage_ref,
    force_ref, first_ref, second_ref, first_half, second_half, taking_ref, sides_send, sides_recv, ends_send, ends_recv,
    halo_ref, send_sem, recv_sem, own_sem, rsend_sem, rrecv_sem, rown_sem, load_sem, block_sem,
    hsend_sem, hrecv_sem,
):
    devices = rows_grid * columns_grid
    total = devices * per_owner
    tiles, _, layers, rows, _ = fluid_ref.shape
    blocks = weights_ref.shape[0]
    groups = rows // 8
    order = [*range(1, groups - 1), groups - 1, 0]
    pairs = [tuple(order[n:n + 2]) for n in range(0, groups, 2)]
    stride = first_ref.shape[3]
    flat_shape = (3, tiles, layers * stride, LANES)

    def block(b):
        return pltpu.make_async_copy(weights_ref.at[b], loaded_ref.at[b], block_sem.at[b])

    def load(t):
        return pltpu.make_async_copy(
            velocity_ref.at[:, :, :, pl.ds(t * LANES, LANES)], fluid_ref.at[t], load_sem.at[t])

    small = [
        pltpu.make_async_copy(source, target, small_sem.at[n])
        for n, (source, target) in enumerate((
            (points_in, points_ref), (stiffness_in, stiffness_ref), (links_in, links_ref),
            (owners_in, owners_ref), (slots_in, slots_ref)))
    ]
    for copy in small:
        copy.start()
    for b in range(blocks):
        block(b).start()
    for t in range(tiles):
        load(t).start()

    gx, gy = lax.axis_index("gx"), lax.axis_index("gy")
    me = gx * columns_grid + gy
    barrier = pltpu.get_barrier_semaphore()

    def hello(off, carry):
        other = lax.rem(me + off, devices)
        pl.semaphore_signal(
            barrier, inc=1, device_id=place(other, columns_grid), device_id_type=MESH)
        return carry

    lax.fori_loop(1, devices, hello, 0)
    for copy in small:
        copy.wait()
    spread(
        devices, per_owner, points_ref, stiffness_ref, links_ref, owners_ref, slots_ref,
        loaded_ref, out_ref, outtable_ref, contrib_ref, stage_ref, lambda b: block(b).wait())
    pl.semaphore_wait(barrier, devices - 1)
    wait = start_swap(
        columns_grid, devices, [out_ref, outtable_ref], [received_ref, table_ref],
        send_sem, recv_sem, own_sem)
    for t in range(tiles):
        load(t).wait()
    wait()

    stage_ref[...] = received_ref[...].astype(F32).reshape(stage_ref.shape)
    for c in range(3):
        force_ref[c] = (force_step * unpack(stage_ref, devices, per_owner, tiles, c)).astype(BF16)
    slots_row = table_row(table_ref, devices, per_owner)
    chunk = 8
    cells = chunk * rows
    lane = iota((16, LANES), 1)
    at_first, at_last = lane == 0, lane == LANES - 1

    def gather_end(side, z, k, value, total_so_far):
        j = z * len(pairs) + k
        shift = j if side == 0 else lax.rem(j + 1, LANES)
        return jnp.where(lane == j, pltpu.roll(value, shift, 1), total_so_far)

    zero = jnp.zeros((16, LANES), BF16)

    def settle(n, ends):
        ends = list(ends)
        placing = one_hot(iota((cells, total), 0) + n * cells == slots_row)
        for c in range(3):
            push = jnp.dot(placing, force_ref[c], preferred_element_type=F32)
            for k in range(chunk):
                z = n * chunk + k
                for t in range(tiles):
                    value = fluid_ref[t, c, z] + push[
                        k * rows:(k + 1) * rows, t * LANES:(t + 1) * LANES]
                    first_ref[c, t, z, PAD:PAD + rows, :] = value
                    for n_pair, pair in enumerate(pairs):
                        packed = jnp.concatenate(
                            [value[8 * g:8 * g + 8] for g in pair], axis=0).astype(BF16)
                        first_half[c, t, z, 16 * n_pair:16 * n_pair + 16, :] = packed
                        for side in range(2):
                            if t == side * (tiles - 1):
                                n_end = side * 3 + c
                                ends[n_end] = gather_end(
                                    side, z, n_pair, packed, ends[n_end])
        return tuple(ends)

    has = [gx > 0, gx < rows_grid - 1, gy > 0, gy < columns_grid - 1]

    def copies_of(step, wanted=range(4)):
        plan = [
            (sides_send.at[step, 0], sides_recv.at[step, 1], (-1, 0), has[0], has[1]),
            (sides_send.at[step, 1], sides_recv.at[step, 0], (1, 0), has[1], has[0]),
            (ends_send.at[step, 0], ends_recv.at[step, 1], (0, -1), has[2], has[3]),
            (ends_send.at[step, 1], ends_recv.at[step, 0], (0, 1), has[3], has[2]),
        ]
        out = []
        for n, (source, target, (dx, dy), sends, receives) in enumerate(plan):
            if n not in wanted:
                continue
            to = (lax.rem(gx + dx + rows_grid, rows_grid),
                  lax.rem(gy + dy + columns_grid, columns_grid))
            out.append((pltpu.make_async_remote_copy(
                src_ref=source, dst_ref=target, send_sem=hsend_sem.at[step, n],
                recv_sem=hrecv_sem.at[step, n], device_id=to, device_id_type=MESH),
                sends, receives))
        return out

    def send_halo(step, ref, ends):
        flat = ref.reshape(flat_shape)
        for side in range(2):
            row = PAD + side * (rows - 1)
            for c in range(3):
                for t in range(tiles):
                    sides_send[step, side, c, t] = jnp.concatenate(
                        [flat[c, t, pl.ds(g * stride + row, 8, stride=stride), :]
                         for g in range(0, layers, 8)], axis=0).astype(BF16)
        for side in range(2):
            for c in range(3):
                ends_send[step, side, c] = ends[side * 3 + c]
        for copy, sends, _ in copies_of(step):
            @pl.when(sends)
            def _():
                copy.start()

    def wait_ends(step):
        for copy, _, receives in copies_of(step, (2, 3)):
            @pl.when(receives)
            def _():
                copy.wait_recv()
        for side in range(2):
            for c in range(3):
                halo_ref[side, c] = jnp.where(
                    has[2 + side], ends_recv[step, side, c].astype(F32), 0.0).astype(BF16)

    def wait_sides(step, ref):
        flat = ref.reshape(flat_shape)
        for copy, _, receives in copies_of(step, (0, 1)):
            @pl.when(receives)
            def _():
                copy.wait_recv()
        for side in range(2):
            row = PAD - 1 if side == 0 else PAD + rows
            for c in range(3):
                for t in range(tiles):
                    value = jnp.where(has[side], sides_recv[step, side, c, t].astype(F32), 0.0)
                    for g in range(0, layers, 8):
                        flat[c, t, pl.ds(g * stride + row, 8, stride=stride), :] = value[g:g + 8]

    def sweep_tiles(ref, half, z, k):
        up, down = lax.rem(z + 1, layers), lax.rem(z + layers - 1, layers)
        j = z * len(pairs) + k
        at = slice(16 * k, 16 * k + 16)

        def beside(c, t, offset):
            return jnp.concatenate(
                [ref[c, t, z, PAD + 8 * g + offset:PAD + 8 * g + offset + 8, :]
                 for g in pairs[k]], axis=0)

        whole = [[beside(c, t, 0) for t in range(tiles)] for c in range(3)]
        mids = [[v.astype(BF16) for v in row] for row in whole]
        right, left = [], []
        for c in range(3):
            right.append([pltpu.roll(halo_ref[0, c], lax.rem(LANES - j, LANES), 1)]
                         + [pltpu.roll(v, 1, 1) for v in mids[c]])
            left.append([pltpu.roll(v, LANES - 1, 1) for v in mids[c]]
                        + [pltpu.roll(halo_ref[1, c], LANES - 1 - j, 1)])
        for t in range(tiles):
            parts = []
            for c in range(3):
                parts.append((
                    mids[c][t], beside(c, t, 1).astype(BF16), beside(c, t, -1).astype(BF16),
                    jnp.where(at_last, left[c][t + 1], left[c][t]),
                    jnp.where(at_first, right[c][t], right[c][t + 1]),
                    half[c, t, up, at, :], half[c, t, down, at, :]))
            change = sweep(*[list(v) for v in zip(*parts)])
            yield t, [keep * whole[c][t] + transport_rate * change[c].astype(F32)
                      for c in range(3)]

    def run(step, ref, half, store, ends):
        def body(wanted, i, ends):
            ends = list(ends)
            for m in range(unroll):
                z = i * unroll + m
                for k in wanted:
                    for t, new in sweep_tiles(ref, half, z, k):
                        for c in range(3):
                            packed = store(c, t, z, k, new[c])
                            if step == 0 and t in (0, tiles - 1):
                                n_end = (0 if t == 0 else 3) + c
                                ends[n_end] = gather_end(t > 0, z, k, packed, ends[n_end])
            return tuple(ends)

        count = layers // unroll
        wait_ends(step)
        ends = lax.fori_loop(
            0, count, functools.partial(body, range(len(pairs) - 1)), ends)
        wait_sides(step, ref)
        return lax.fori_loop(0, count, functools.partial(body, (len(pairs) - 1,)), ends)

    ends = lax.fori_loop(0, layers // chunk, settle, (zero,) * 6)
    send_halo(0, first_ref, ends)
    slots = table_column(table_ref, per_owner)
    taking_ref[...] = one_hot(iota((total, layers * rows), 1) == slots)

    def store_first(c, t, z, k, value):
        for m, g in enumerate(pairs[k]):
            second_ref[c, t, z, PAD + 8 * g:PAD + 8 * g + 8, :] = value[8 * m:8 * m + 8]
        packed = value.astype(BF16)
        second_half[c, t, z, 16 * k:16 * k + 16, :] = packed
        return packed

    ends = run(0, first_ref, first_half, store_first, (zero,) * 6)
    send_halo(1, second_ref, ends)

    def store_second(c, t, z, k, value):
        for m, g in enumerate(pairs[k]):
            fluid_ref[t, c, z, 8 * g:8 * g + 8, :] = value[8 * m:8 * m + 8]

    run(1, second_ref, second_half, store_second, (zero,) * 6)

    width = 3 * tiles * per_owner
    for c in range(3):
        for h in range(0, tiles, 2):
            flat = jnp.concatenate(
                [fluid_ref[h + s, c].reshape(layers * rows, LANES).astype(BF16)
                 for s in range(2)], axis=1)
            part = jnp.dot(taking_ref[...], flat, preferred_element_type=F32)
            for p in range(per_owner):
                for s in range(2):
                    stage_ref[pl.ds(p * 3 * tiles + c * tiles + h + s, devices, stride=width), :] = (
                        part[p * devices:(p + 1) * devices, s * LANES:(s + 1) * LANES])
    replies_ref[...] = stage_ref[...].reshape(replies_ref.shape).astype(BF16)
    wait = start_swap(
        columns_grid, devices, [replies_ref], [returned_ref], rsend_sem, rrecv_sem, rown_sem)
    for step in range(STEPS):
        for copy, sends, _ in copies_of(step):
            @pl.when(sends)
            def _():
                copy.wait_send()
    owner_row = to_row(owners_ref[:, 0, :])
    places = slot_column(owner_row, to_column(owner_row), devices)
    selector = one_hot(iota((places.shape[0], total), 1) == places)
    wait()
    interpolate(
        devices, per_owner, returned_ref, loaded_ref, selector, stage_ref, picked_ref, interp_ref)


def interpolate(
    devices, per_owner, returned_ref, loaded_ref, selector, stage_ref, picked_ref, interp_ref,
):
    blocks, k, points, patch = loaded_ref.shape
    tiles = patch // LANES
    stage_ref[...] = returned_ref[...].astype(F32).reshape(stage_ref.shape)
    for c in range(3):
        replies = unpack(stage_ref, devices, per_owner, tiles, c).astype(BF16)
        picked_ref[c] = jnp.dot(selector, replies, preferred_element_type=F32)
    diagonal = iota((k, k * points), 0) == iota((k, k * points), 1) // points
    for b in range(blocks):
        rows = [picked_ref[c, b * k:(b + 1) * k, :] for c in range(3)]
        rows.append(jnp.zeros_like(rows[0]))
        left = jnp.concatenate(rows, axis=0).astype(BF16)
        right = loaded_ref[b].reshape(k * points, patch)
        result = lax.dot_general(
            left, right, (((1,), (1,)), ((), ())), preferred_element_type=F32)
        for c in range(3):
            own = jnp.where(diagonal, result[c * k:(c + 1) * k], 0.0)
            fold = own[:, 0:points]
            for n in range(1, k):
                fold = fold + own[:, n * points:(n + 1) * points]
            interp_ref[c, b:b + 1, :] = jnp.sum(fold, axis=0, keepdims=True)


def finish_kernel(fluid_ref, interp_ref, points_ref, out_ref, moved_ref, store_sem):
    def store(t):
        return pltpu.make_async_copy(
            fluid_ref.at[t], out_ref.at[:, :, :, pl.ds(t * LANES, LANES)], store_sem.at[t])

    for t in range(fluid_ref.shape[0]):
        store(t).start()
    moved_ref[...] = points_ref[...] + fiber_step * interp_ref[...]
    for t in range(fluid_ref.shape[0]):
        store(t).wait()


def shards(rows_grid, columns_grid, velocity, fiber_points, stiffness, links, delta_weights,
           owners, patch_slots):
    blocks, intersection, points, patch = delta_weights.shape
    _, layers, rows, columns = velocity.shape
    devices = rows_grid * columns_grid
    entries = blocks * intersection
    per_owner = max(2, (2 * entries + devices - 1) // devices)
    total = devices * per_owner
    tiles = patch // LANES
    width = 3 * tiles * per_owner
    owners = jnp.transpose(owners, (0, 2, 1))
    points_first = jnp.transpose(fiber_points, (1, 0, 2))
    message = jax.ShapeDtypeStruct((devices, width, LANES), BF16)
    table_shape = jax.ShapeDtypeStruct((devices, 1, LANES), I32)
    stage = pltpu.VMEM((devices * width, LANES), F32)
    limit = 46 << 20
    field = pltpu.VMEM((3, tiles, layers, rows + 2 * PAD, LANES), F32)
    half = pltpu.VMEM((3, tiles, layers, rows, LANES), BF16)
    sides = pltpu.VMEM((STEPS, 2, 3, tiles, layers, LANES), BF16)
    ends = pltpu.VMEM((STEPS, 2, 3, 16, LANES), BF16)
    fluid_tiles, interp = pl.pallas_call(
        functools.partial(step_kernel, rows_grid, columns_grid, per_owner, UNROLL),
        out_shape=[
            jax.ShapeDtypeStruct((tiles, 3, layers, rows, LANES), F32),
            jax.ShapeDtypeStruct(points_first.shape, F32),
        ],
        in_specs=[HBM] * 7,
        out_specs=[VMEM] * 2,
        scratch_shapes=[
            pltpu.VMEM(delta_weights.shape, BF16),
            pltpu.VMEM(message.shape, BF16),
            pltpu.VMEM((3, entries, patch), F32),
            pltpu.VMEM(points_first.shape, F32),
            pltpu.SMEM(stiffness.shape, F32),
            pltpu.VMEM(links.shape, I32),
            pltpu.VMEM(owners.shape, I32),
            pltpu.VMEM(patch_slots.shape, I32),
            pltpu.SemaphoreType.DMA((5,)),
            pltpu.VMEM(message.shape, BF16),
            pltpu.VMEM(table_shape.shape, I32),
            pltpu.VMEM(message.shape, BF16),
            pltpu.VMEM(table_shape.shape, I32),
            pltpu.VMEM(message.shape, BF16),
            pltpu.VMEM((3, entries, patch), F32),
            stage,
            pltpu.VMEM((3, total, patch), BF16),
            field, field, half, half,
            pltpu.VMEM((total, layers * rows), BF16),
            sides, sides, ends, ends,
            pltpu.VMEM((2, 3, 16, LANES), BF16),
            *swap_sems(2, devices),
            *swap_sems(1, devices),
            pltpu.SemaphoreType.DMA((tiles,)),
            pltpu.SemaphoreType.DMA((blocks,)),
            pltpu.SemaphoreType.DMA((STEPS, 4)),
            pltpu.SemaphoreType.DMA((STEPS, 4)),
        ],
        compiler_params=pltpu.CompilerParams(
            collective_id=0, has_side_effects=True, vmem_limit_bytes=limit),
    )(*[pltpu.with_memory_space_constraint(v, pltpu.HBM) for v in (
        points_first, stiffness, links, owners, patch_slots, delta_weights, velocity)])

    fluid, moved = pl.pallas_call(
        finish_kernel,
        out_shape=[
            jax.ShapeDtypeStruct(velocity.shape, F32),
            jax.ShapeDtypeStruct(points_first.shape, F32),
        ],
        in_specs=[VMEM] * 3,
        out_specs=[HBM, VMEM],
        scratch_shapes=[pltpu.SemaphoreType.DMA((tiles,))],
        compiler_params=pltpu.CompilerParams(vmem_limit_bytes=limit),
    )(fluid_tiles, interp, points_first)
    return fluid, jnp.transpose(moved, (1, 0, 2))


def solution(mesh):
    placed = (
        P(None, None, "gx", "gy"),
        P(("gx", "gy"), None, None),
        P(("gx", "gy")),
        P(("gx", "gy"), None),
        P(("gx", "gy"), None, None, None),
        P(("gx", "gy"), None, None),
        P(("gx", "gy"), None),
    )
    return jax.shard_map(
        functools.partial(shards, mesh.shape["gx"], mesh.shape["gy"]),
        mesh=mesh,
        in_specs=placed,
        out_specs=(placed[0], placed[1]),
        check_vma=False,
    )
```

```python
import functools

import jax
import jax.numpy as jnp
from jax import lax
from jax.experimental import pallas as pl
from jax.experimental.pallas import tpu as pltpu
from jax.sharding import PartitionSpec as P

STEPS = 2
viscosity = 0.1
transport_rate = 0.1
force_step = 0.5
fiber_step = 0.25

F32 = jnp.float32
BF16 = jnp.bfloat16
I32 = jnp.int32
LANES = 128
MESH = pl.DeviceIdType.MESH
VMEM = pl.BlockSpec(memory_space=pltpu.VMEM)
ANY = pl.BlockSpec(memory_space=pl.ANY)
SMEM = pl.BlockSpec(memory_space=pltpu.SMEM)


def iota(shape, dim):
    return lax.broadcasted_iota(I32, shape, dim)


def to_column(row):
    n = row.shape[1]
    return jnp.sum(jnp.where(iota((n, n), 0) == iota((n, n), 1), row, 0), axis=1, keepdims=True)


def to_row(grid):
    n, k = grid.shape
    tiled = jnp.concatenate([grid] * n, axis=1)
    return jnp.sum(
        jnp.where(iota((n, n * k), 0) == iota((n, n * k), 1) // k, tiled, 0), axis=0, keepdims=True)


def slot_row(owner_row, owner_column, devices):
    n = owner_row.shape[1]
    same = (owner_column == owner_row) & (iota((n, n), 0) < iota((n, n), 1))
    rank = jnp.sum(jnp.where(same, 1, 0), axis=0, keepdims=True)
    return rank * devices + owner_row


def slot_column(owner_row, owner_column, devices):
    n = owner_row.shape[1]
    same = (owner_column == owner_row) & (iota((n, n), 1) < iota((n, n), 0))
    rank = jnp.sum(jnp.where(same, 1, 0), axis=1, keepdims=True)
    return rank * devices + owner_column


def spread(
    devices, per_owner, points_ref, stiffness_ref, links_ref, owners_ref, slots_ref, loaded_ref,
    out_ref, table_ref, contrib_ref, stage_ref, wait_block,
):
    blocks, k, points, patch = loaded_ref.shape
    parts = []
    for c in range(3):
        rest = points_ref[c]
        for _ in range(3):
            part = rest.astype(BF16).astype(F32)
            parts.append(part)
            rest = rest - part
    parts.append(jnp.zeros_like(parts[0]))
    parts = jnp.concatenate(parts, axis=0).astype(BF16)
    partner = lax.rem(iota(links_ref.shape, 1) + links_ref[...], points)
    diagonal = iota((k, k * points), 0) == iota((k, k * points), 1) // points
    lefts = []
    for b in range(blocks):
        moving = one_hot(iota((points, points), 0) == partner[b:b + 1])
        there = jnp.dot(parts, moving, preferred_element_type=F32)
        rows = []
        for c in range(3):
            r = 3 * c * blocks + b
            found = there[r:r + 1] + there[r + blocks:r + blocks + 1]
            found = found + there[r + 2 * blocks:r + 2 * blocks + 1]
            row = stiffness_ref[b] * (found - points_ref[c, b:b + 1, :])
            rows.append(jnp.where(diagonal, jnp.concatenate([row] * k, axis=1), 0.0))
        rows.append(jnp.zeros_like(rows[0]))
        lefts.append(jnp.concatenate(rows, axis=0).astype(BF16))

    owner_row = to_row(owners_ref[:, 0, :])
    places = slot_row(owner_row, to_column(owner_row), devices)
    total = devices * per_owner
    chosen = iota((total, places.shape[1]), 0) == places
    selector = one_hot(chosen)

    for b in range(blocks):
        wait_block(b)
        right = loaded_ref[b].reshape(k * points, patch)
        result = jnp.dot(lefts[b], right, preferred_element_type=F32)
        for c in range(3):
            contrib_ref[c, b * k:(b + 1) * k, :] = result[c * k:(c + 1) * k]

    tiles = patch // LANES
    width = 3 * tiles * per_owner
    for c in range(3):
        packed = jnp.dot(selector, contrib_ref[c].astype(BF16), preferred_element_type=F32)
        for p in range(per_owner):
            for t in range(tiles):
                stage_ref[pl.ds(p * 3 * tiles + c * tiles + t, devices, stride=width), :] = (
                    packed[p * devices:(p + 1) * devices, t * LANES:(t + 1) * LANES]
                )
    out_ref[...] = stage_ref[...].reshape(out_ref.shape).astype(BF16)
    column = jnp.max(jnp.where(chosen, to_row(slots_ref[...]), -1), axis=1, keepdims=True)
    lane = iota((devices, LANES), 1)
    table = jnp.full((devices, LANES), -1, I32)
    for p in range(per_owner):
        table = jnp.where(lane == p, column[p * devices:(p + 1) * devices], table)
    for d in range(devices):
        table_ref[d] = table[d:d + 1]


HBM = pl.BlockSpec(memory_space=pltpu.HBM)


def each_peer(rows_grid, columns_grid, visit, carry=0):
    gx, gy = lax.axis_index("gx"), lax.axis_index("gy")
    ys = [lax.rem(gy + dy, columns_grid) for dy in range(columns_grid)]
    for dy in range(1, columns_grid):
        visit(dy, (gx, ys[dy]))

    def row(dx, carry):
        x = lax.rem(gx + dx, rows_grid)
        for dy in range(columns_grid):
            visit(dx * columns_grid + dy, (x, ys[dy]))
        return carry

    lax.fori_loop(1, rows_grid, row, 0)


def start_swap(rows_grid, columns_grid, source, target, send_sem, recv_sem):
    devices = rows_grid * columns_grid
    me = lax.axis_index("gx") * columns_grid + lax.axis_index("gy")

    def start(off, to):
        pltpu.make_async_remote_copy(
            src_ref=source.at[to[0] * columns_grid + to[1]], dst_ref=target.at[me],
            send_sem=send_sem, recv_sem=recv_sem, device_id=to, device_id_type=MESH,
        ).start()

    each_peer(rows_grid, columns_grid, start)
    pltpu.make_async_copy(source.at[me], target.at[me], recv_sem).start()

    def wait():
        sent = pl.ds(0, devices - 1)
        pltpu.make_async_copy(source, target, recv_sem).wait()
        pltpu.make_async_copy(source.at[sent], target.at[sent], send_sem).wait()

    return wait


def unpack(stage_ref, devices, per_owner, tiles, c):
    width = 3 * tiles * per_owner
    rows = []
    for p in range(per_owner):
        rows.append(jnp.concatenate(
            [stage_ref[pl.ds(p * 3 * tiles + c * tiles + t, devices, stride=width), :]
             for t in range(tiles)], axis=1))
    return jnp.concatenate(rows, axis=0)


def table_row(table_ref, devices, per_owner):
    total = devices * per_owner
    row = jnp.zeros((1, total), I32)
    for p in range(per_owner):
        column = table_ref[:, 0, :][:, p:p + 1]
        spot = iota((devices, total), 1) == p * devices + iota((devices, total), 0)
        row = row + jnp.sum(jnp.where(spot, column, 0), axis=0, keepdims=True)
    return row


def table_column(table_ref, per_owner):
    return jnp.concatenate([table_ref[:, 0, :][:, p:p + 1] for p in range(per_owner)], axis=0)


def one_hot(mask):
    return mask.astype(F32).astype(BF16)


PAD = 8
UNROLL = 4
assert viscosity == transport_rate
keep = 1.0 - 6.0 * viscosity


def sweep(mid, east, west, north, south, above, below):
    coefficients = [(1 - m, 1 + m) for m in mid]
    out = []
    for c in range(3):
        pairs = [
            ahead * front[c] + behind * back[c]
            for (ahead, behind), (front, back) in zip(
                coefficients, ((east, west), (north, south), (above, below)))
        ]
        out.append(pairs[0] + (pairs[1] + pairs[2]))
    return out


def step_kernel(
    rows_grid, columns_grid, per_owner, points_in, stiffness_in, links_in, owners_in,
    slots_in, weights_ref, velocity_ref,
    fluid_ref, loaded_ref, returned_ref,
    points_ref, stiffness_ref, links_ref, owners_ref, slots_ref, small_sem, received_ref, table_ref, out_ref, outtable_ref, replies_ref, contrib_ref, stage_ref,
    force_ref, first_ref, second_ref, first_half, second_half, taking_ref, sides_send, sides_recv, ends_send, ends_recv,
    halo_ref, send_sem, recv_sem, load_sem, block_sem,
    hsend_sem, hrecv_sem,
):
    devices = rows_grid * columns_grid
    total = devices * per_owner
    tiles, _, layers, rows, _ = fluid_ref.shape
    blocks = weights_ref.shape[0]
    groups = rows // 8
    order = [*range(1, groups - 1), groups - 1, 0]
    pairs = [tuple(order[n:n + 2]) for n in range(0, groups, 2)]
    stride = first_ref.shape[3]
    flat_shape = (3, tiles, layers * stride, LANES)

    def block(b):
        return pltpu.make_async_copy(weights_ref.at[b], loaded_ref.at[b], block_sem.at[b])

    def load(t):
        return pltpu.make_async_copy(
            velocity_ref.at[:, :, :, pl.ds(t * LANES, LANES)], fluid_ref.at[t], load_sem.at[t])

    small = [
        pltpu.make_async_copy(source, target, small_sem.at[n])
        for n, (source, target) in enumerate((
            (points_in, points_ref), (stiffness_in, stiffness_ref), (links_in, links_ref),
            (owners_in, owners_ref), (slots_in, slots_ref)))
    ]
    for copy in small:
        copy.start()
    for b in range(blocks):
        block(b).start(priority=1)

    def wait_block(b):
        block(b).wait()
        if b == blocks - 1:
            for t in range(tiles):
                load(t).start()

    gx, gy = lax.axis_index("gx"), lax.axis_index("gy")
    barrier = pltpu.get_barrier_semaphore()

    def hello(off, to):
        pl.semaphore_signal(barrier, inc=1, device_id=to, device_id_type=MESH)

    each_peer(rows_grid, columns_grid, hello)
    for copy in small:
        copy.wait()
    spread(
        devices, per_owner, points_ref, stiffness_ref, links_ref, owners_ref, slots_ref,
        loaded_ref, out_ref, outtable_ref, contrib_ref, stage_ref, wait_block)
    pl.semaphore_wait(barrier, devices - 1)
    wait_table = start_swap(
        rows_grid, columns_grid, outtable_ref, table_ref, send_sem.at[0], recv_sem.at[0])
    wait = start_swap(
        rows_grid, columns_grid, out_ref, received_ref, send_sem.at[1], recv_sem.at[1])
    for t in range(tiles):
        load(t).wait()
    wait_table()
    wait()

    stage_ref[...] = received_ref[...].astype(F32).reshape(stage_ref.shape)
    for c in range(3):
        force_ref[c] = (force_step * unpack(stage_ref, devices, per_owner, tiles, c)).astype(BF16)
    slots_row = table_row(table_ref, devices, per_owner)
    chunk = 8
    cells = chunk * rows
    lane = iota((16, LANES), 1)
    at_first, at_last = lane == 0, lane == LANES - 1

    unit = one_hot(at_first)

    def gather_end(side, mark, j, value, total_so_far):
        shift = j if side == 0 else lax.rem(j + 1, LANES)
        return total_so_far + mark * pltpu.roll(value, shift, 1)

    zero = jnp.zeros((16, LANES), BF16)

    def settle(n, ends):
        ends = list(ends)
        placing = one_hot(iota((cells, total), 0) + n * cells == slots_row)
        for c in range(3):
            push = jnp.dot(placing, force_ref[c], preferred_element_type=F32)
            for k in range(chunk):
                z = n * chunk + k
                for t in range(tiles):
                    value = fluid_ref[t, c, z] + push[
                        k * rows:(k + 1) * rows, t * LANES:(t + 1) * LANES]
                    first_ref[c, t, z, PAD:PAD + rows, :] = value
                    for n_pair, pair in enumerate(pairs):
                        packed = jnp.concatenate(
                            [value[8 * g:8 * g + 8] for g in pair], axis=0).astype(BF16)
                        first_half[c, t, z, 16 * n_pair:16 * n_pair + 16, :] = packed
                        for side in range(2):
                            if t == side * (tiles - 1):
                                n_end = side * 3 + c
                                j = z * len(pairs) + n_pair
                                ends[n_end] = gather_end(
                                    side, pltpu.roll(unit, j, 1), j, packed, ends[n_end])
        return tuple(ends)

    has = [gx > 0, gx < rows_grid - 1, gy > 0, gy < columns_grid - 1]

    def copies_of(step, wanted=range(4)):
        plan = [
            (sides_send.at[step, 0], sides_recv.at[step, 1], (-1, 0), has[0], has[1]),
            (sides_send.at[step, 1], sides_recv.at[step, 0], (1, 0), has[1], has[0]),
            (ends_send.at[step, 0], ends_recv.at[step, 1], (0, -1), has[2], has[3]),
            (ends_send.at[step, 1], ends_recv.at[step, 0], (0, 1), has[3], has[2]),
        ]
        out = []
        for n, (source, target, (dx, dy), sends, receives) in enumerate(plan):
            if n not in wanted:
                continue
            to = (lax.rem(gx + dx + rows_grid, rows_grid),
                  lax.rem(gy + dy + columns_grid, columns_grid))
            out.append((pltpu.make_async_remote_copy(
                src_ref=source, dst_ref=target, send_sem=hsend_sem.at[step, n],
                recv_sem=hrecv_sem.at[step, n], device_id=to, device_id_type=MESH),
                sends, receives))
        return out

    def send_halo(step, ref, ends):
        flat = ref.reshape(flat_shape)
        for side in range(2):
            row = PAD + side * (rows - 1)
            for c in range(3):
                for t in range(tiles):
                    sides_send[step, side, c, t] = jnp.concatenate(
                        [flat[c, t, pl.ds(g * stride + row, 8, stride=stride), :]
                         for g in range(0, layers, 8)], axis=0).astype(BF16)
        for side in range(2):
            for c in range(3):
                ends_send[step, side, c] = ends[side * 3 + c]
        for copy, sends, _ in copies_of(step):
            @pl.when(sends)
            def _():
                copy.start()

    def wait_ends(step):
        for copy, _, receives in copies_of(step, (2, 3)):
            @pl.when(receives)
            def _():
                copy.wait_recv()
        for side in range(2):
            for c in range(3):
                halo_ref[side, c] = jnp.where(
                    has[2 + side], ends_recv[step, side, c].astype(F32), 0.0).astype(BF16)

    def wait_sides(step, ref):
        flat = ref.reshape(flat_shape)
        for copy, _, receives in copies_of(step, (0, 1)):
            @pl.when(receives)
            def _():
                copy.wait_recv()
        for side in range(2):
            row = PAD - 1 if side == 0 else PAD + rows
            for c in range(3):
                for t in range(tiles):
                    value = jnp.where(has[side], sides_recv[step, side, c, t].astype(F32), 0.0)
                    for g in range(0, layers, 8):
                        flat[c, t, pl.ds(g * stride + row, 8, stride=stride), :] = value[g:g + 8]

    def sweep_tiles(ref, half, z, k, wanted):
        up, down = lax.rem(z + 1, layers), lax.rem(z + layers - 1, layers)
        j = z * len(pairs) + k
        at = slice(16 * k, 16 * k + 16)

        def beside(c, t, offset):
            return jnp.concatenate(
                [ref[c, t, z, PAD + 8 * g + offset:PAD + 8 * g + offset + 8, :]
                 for g in pairs[k]], axis=0)

        whole = [[beside(c, t, 0) for t in range(tiles)] for c in range(3)]
        mids = [[v.astype(BF16) for v in row] for row in whole]
        turned = {}

        def turn(c, t, shift):
            if (c, t, shift) not in turned:
                if t < 0:
                    v = pltpu.roll(halo_ref[0, c], lax.rem(LANES - j, LANES), 1)
                elif t == tiles:
                    v = pltpu.roll(halo_ref[1, c], LANES - 1 - j, 1)
                else:
                    v = pltpu.roll(mids[c][t], shift, 1)
                turned[c, t, shift] = v
            return turned[c, t, shift]

        for t in wanted:
            parts = []
            for c in range(3):
                parts.append((
                    mids[c][t], beside(c, t, 1).astype(BF16), beside(c, t, -1).astype(BF16),
                    jnp.where(at_last, turn(c, t + 1, LANES - 1), turn(c, t, LANES - 1)),
                    jnp.where(at_first, turn(c, t - 1, 1), turn(c, t, 1)),
                    half[c, t, up, at, :], half[c, t, down, at, :]))
            change = sweep(*[list(v) for v in zip(*parts)])
            yield t, [keep * whole[c][t] + transport_rate * change[c].astype(F32)
                      for c in range(3)]

    def run(ref, half, store, edge, groups_wanted, tiles_wanted, unroll, ends):
        def body(i, ends):
            ends = list(ends)
            for m in range(unroll):
                z = i * unroll + m
                for k in groups_wanted:
                    j = z * len(pairs) + k
                    mark = pltpu.roll(unit, j, 1)
                    for t, new in sweep_tiles(ref, half, z, k, tiles_wanted):
                        for c in range(3):
                            packed = store(c, t, z, k, new[c])
                            if edge and t in (0, tiles - 1):
                                n_end = (0 if t == 0 else 3) + c
                                ends[n_end] = gather_end(t > 0, mark, j, packed, ends[n_end])
            return tuple(ends)

        return lax.fori_loop(0, layers // unroll, body, ends)

    inner, outer = range(len(pairs) - 1), (len(pairs) - 1,)
    every = range(tiles)
    ends_zero = (zero,) * 6
    ends = lax.fori_loop(0, layers // chunk, settle, (zero,) * 6)
    send_halo(0, first_ref, ends)
    slots = table_column(table_ref, per_owner)
    taking_ref[...] = one_hot(iota((total, layers * rows), 1) == slots)

    def store_first(c, t, z, k, value):
        for m, g in enumerate(pairs[k]):
            second_ref[c, t, z, PAD + 8 * g:PAD + 8 * g + 8, :] = value[8 * m:8 * m + 8]
        packed = value.astype(BF16)
        second_half[c, t, z, 16 * k:16 * k + 16, :] = packed
        return packed

    wait_ends(0)
    ends = run(first_ref, first_half, store_first, True, inner, every, UNROLL, ends_zero)
    wait_sides(0, first_ref)
    ends = run(first_ref, first_half, store_first, True, outer, every, UNROLL, ends)
    send_halo(1, second_ref, ends)

    def store_second(c, t, z, k, value):
        for m, g in enumerate(pairs[k]):
            fluid_ref[t, c, z, 8 * g:8 * g + 8, :] = value[8 * m:8 * m + 8]

    half_tiles = tiles // 2
    wide = replies_ref.shape[2]
    wait_ends(1)
    waits = []
    for h in range(2):
        mine = range(h * half_tiles, (h + 1) * half_tiles)
        run(second_ref, second_half, store_second, False, inner, mine, 2 * UNROLL, ())
        if h == 0:
            wait_sides(1, second_ref)
        run(second_ref, second_half, store_second, False, outer, mine, 2 * UNROLL, ())
        for c in range(3):
            flat = jnp.concatenate(
                [fluid_ref[t, c].reshape(layers * rows, LANES).astype(BF16) for t in mine], axis=1)
            part = jnp.dot(taking_ref[...], flat, preferred_element_type=F32)
            for p in range(per_owner):
                for n in range(half_tiles):
                    row = (p * 3 + c) * half_tiles + n
                    stage_ref[pl.ds(row, devices, stride=wide), :] = (
                        part[p * devices:(p + 1) * devices, n * LANES:(n + 1) * LANES])
        replies_ref[h] = stage_ref[0:devices * wide, :].reshape(replies_ref.shape[1:]).astype(BF16)
        waits.append(start_swap(
            rows_grid, columns_grid, replies_ref.at[h], returned_ref.at[h],
            send_sem.at[2 + h], recv_sem.at[2 + h]))
    for step in range(STEPS):
        for copy, sends, _ in copies_of(step):
            @pl.when(sends)
            def _():
                copy.wait_send()
    for wait in waits:
        wait()


def interpolate(
    devices, per_owner, returned_ref, loaded_ref, selector, stage_ref, picked_ref, points_ref, moved_ref,
):
    blocks, k, points, patch = loaded_ref.shape
    tiles = patch // LANES
    half_tiles = tiles // 2
    wide = returned_ref.shape[2]
    for h in range(2):
        stage_ref[0:devices * wide, :] = returned_ref[h].astype(F32).reshape(
            devices * wide, LANES)
        for c in range(3):
            replies = jnp.concatenate(
                [jnp.concatenate(
                    [stage_ref[pl.ds((p * 3 + c) * half_tiles + n, devices, stride=wide), :]
                     for n in range(half_tiles)], axis=1)
                 for p in range(per_owner)], axis=0).astype(BF16)
            picked_ref[c, :, h * half_tiles * LANES:(h + 1) * half_tiles * LANES] = jnp.dot(
                selector, replies, preferred_element_type=F32)
    diagonal = iota((k, k * points), 0) == iota((k, k * points), 1) // points
    for b in range(blocks):
        rows = [picked_ref[c, b * k:(b + 1) * k, :] for c in range(3)]
        rows.append(jnp.zeros_like(rows[0]))
        left = jnp.concatenate(rows, axis=0).astype(BF16)
        right = loaded_ref[b].reshape(k * points, patch)
        result = lax.dot_general(
            left, right, (((1,), (1,)), ((), ())), preferred_element_type=F32)
        for c in range(3):
            own = jnp.where(diagonal, result[c * k:(c + 1) * k], 0.0)
            fold = own[:, 0:points]
            for n in range(1, k):
                fold = fold + own[:, n * points:(n + 1) * points]
            interp = jnp.sum(fold, axis=0, keepdims=True)
            moved_ref[c, b:b + 1, :] = points_ref[c, b:b + 1, :] + fiber_step * interp


def finish_kernel(
    devices, per_owner, fluid_ref, loaded_ref, returned_ref, owners_in, points_in,
    out_ref, moved_ref, owners_ref, points_ref, stage_ref, picked_ref, small_sem, store_sem,
):
    def store(t):
        return pltpu.make_async_copy(
            fluid_ref.at[t], out_ref.at[:, :, :, pl.ds(t * LANES, LANES)], store_sem.at[t])

    small = [
        pltpu.make_async_copy(owners_in, owners_ref, small_sem.at[0]),
        pltpu.make_async_copy(points_in, points_ref, small_sem.at[1]),
    ]
    for copy in small:
        copy.start()
    for t in range(fluid_ref.shape[0]):
        store(t).start()
    for copy in small:
        copy.wait()
    owner_row = to_row(owners_ref[:, 0, :])
    places = slot_column(owner_row, to_column(owner_row), devices)
    selector = one_hot(iota((places.shape[0], devices * per_owner), 1) == places)
    interpolate(
        devices, per_owner, returned_ref, loaded_ref, selector, stage_ref, picked_ref, points_ref,
        moved_ref)
    for t in range(fluid_ref.shape[0]):
        store(t).wait()


def shards(rows_grid, columns_grid, velocity, fiber_points, stiffness, links, delta_weights,
           owners, patch_slots):
    blocks, intersection, points, patch = delta_weights.shape
    _, layers, rows, columns = velocity.shape
    devices = rows_grid * columns_grid
    entries = blocks * intersection
    per_owner = max(2, (2 * entries + devices - 1) // devices)
    total = devices * per_owner
    tiles = patch // LANES
    width = 3 * tiles * per_owner
    owners = jnp.transpose(owners, (0, 2, 1))
    points_first = jnp.transpose(fiber_points, (1, 0, 2))
    message = jax.ShapeDtypeStruct((devices, width, LANES), BF16)
    wide = -(-3 * (tiles // 2) * per_owner // 8) * 8
    reply = jax.ShapeDtypeStruct((2, devices, wide, LANES), BF16)
    table_shape = jax.ShapeDtypeStruct((devices, 1, LANES), I32)
    stage = pltpu.VMEM((devices * max(width, wide), LANES), F32)
    limit = 32 << 20
    field = pltpu.VMEM((3, tiles, layers, rows + 2 * PAD, LANES), F32)
    half = pltpu.VMEM((3, tiles, layers, rows, LANES), BF16)
    sides = pltpu.VMEM((STEPS, 2, 3, tiles, layers, LANES), BF16)
    ends = pltpu.VMEM((STEPS, 2, 3, 16, LANES), BF16)
    fluid_tiles, weights, returned = pl.pallas_call(
        functools.partial(step_kernel, rows_grid, columns_grid, per_owner),
        out_shape=[
            jax.ShapeDtypeStruct((tiles, 3, layers, rows, LANES), F32),
            jax.ShapeDtypeStruct(delta_weights.shape, BF16),
            reply,
        ],
        in_specs=[HBM] * 7,
        out_specs=[VMEM] * 3,
        scratch_shapes=[
            pltpu.VMEM(points_first.shape, F32),
            pltpu.SMEM(stiffness.shape, F32),
            pltpu.VMEM(links.shape, I32),
            pltpu.VMEM(owners.shape, I32),
            pltpu.VMEM(patch_slots.shape, I32),
            pltpu.SemaphoreType.DMA((5,)),
            pltpu.VMEM(message.shape, BF16),
            pltpu.VMEM(table_shape.shape, I32),
            pltpu.VMEM(message.shape, BF16),
            pltpu.VMEM(table_shape.shape, I32),
            pltpu.VMEM(reply.shape, BF16),
            pltpu.VMEM((3, entries, patch), F32),
            stage,
            pltpu.VMEM((3, total, patch), BF16),
            field, field, half, half,
            pltpu.VMEM((total, layers * rows), BF16),
            sides, sides, ends, ends,
            pltpu.VMEM((2, 3, 16, LANES), BF16),
            pltpu.SemaphoreType.DMA((4,)),
            pltpu.SemaphoreType.DMA((4,)),
            pltpu.SemaphoreType.DMA((tiles,)),
            pltpu.SemaphoreType.DMA((blocks,)),
            pltpu.SemaphoreType.DMA((STEPS, 4)),
            pltpu.SemaphoreType.DMA((STEPS, 4)),
        ],
        compiler_params=pltpu.CompilerParams(
            collective_id=0, has_side_effects=True, vmem_limit_bytes=limit),
    )(*[pltpu.with_memory_space_constraint(v, pltpu.HBM) for v in (
        points_first, stiffness, links, owners, patch_slots, delta_weights, velocity)])

    fluid, moved = pl.pallas_call(
        functools.partial(finish_kernel, devices, per_owner),
        out_shape=[
            jax.ShapeDtypeStruct(velocity.shape, F32),
            jax.ShapeDtypeStruct(points_first.shape, F32),
        ],
        in_specs=[VMEM, VMEM, VMEM, HBM, HBM],
        out_specs=[HBM, VMEM],
        scratch_shapes=[
            pltpu.VMEM(owners.shape, I32),
            pltpu.VMEM(points_first.shape, F32),
            stage,
            pltpu.VMEM((3, entries, patch), F32),
            pltpu.SemaphoreType.DMA((2,)),
            pltpu.SemaphoreType.DMA((tiles,)),
        ],
        compiler_params=pltpu.CompilerParams(vmem_limit_bytes=8 << 20),
    )(fluid_tiles, weights, returned, pltpu.with_memory_space_constraint(owners, pltpu.HBM),
      pltpu.with_memory_space_constraint(points_first, pltpu.HBM))
    return fluid, jnp.transpose(moved, (1, 0, 2))


def solution(mesh):
    placed = (
        P(None, None, "gx", "gy"),
        P(("gx", "gy"), None, None),
        P(("gx", "gy")),
        P(("gx", "gy"), None),
        P(("gx", "gy"), None, None, None),
        P(("gx", "gy"), None, None),
        P(("gx", "gy"), None),
    )
    return jax.shard_map(
        functools.partial(shards, mesh.shape["gx"], mesh.shape["gy"]),
        mesh=mesh,
        in_specs=placed,
        out_specs=(placed[0], placed[1]),
        check_vma=False,
    )
```

```python
import functools

import jax
import jax.numpy as jnp
from jax import lax
from jax.experimental import pallas as pl
from jax.experimental.pallas import tpu as pltpu
from jax.sharding import PartitionSpec as P

STEPS = 2
viscosity = 0.1
transport_rate = 0.1
force_step = 0.5
fiber_step = 0.25

F32 = jnp.float32
BF16 = jnp.bfloat16
I32 = jnp.int32
LANES = 128
MESH = pl.DeviceIdType.MESH
VMEM = pl.BlockSpec(memory_space=pltpu.VMEM)
ANY = pl.BlockSpec(memory_space=pl.ANY)
SMEM = pl.BlockSpec(memory_space=pltpu.SMEM)


def iota(shape, dim):
    return lax.broadcasted_iota(I32, shape, dim)


def to_column(row):
    n = row.shape[1]
    return jnp.sum(jnp.where(iota((n, n), 0) == iota((n, n), 1), row, 0), axis=1, keepdims=True)


def to_row(grid):
    n, k = grid.shape
    tiled = jnp.concatenate([grid] * n, axis=1)
    return jnp.sum(
        jnp.where(iota((n, n * k), 0) == iota((n, n * k), 1) // k, tiled, 0), axis=0, keepdims=True)


def slot_row(owner_row, owner_column, devices):
    n = owner_row.shape[1]
    same = (owner_column == owner_row) & (iota((n, n), 0) < iota((n, n), 1))
    rank = jnp.sum(jnp.where(same, 1, 0), axis=0, keepdims=True)
    return rank * devices + owner_row


def slot_column(owner_row, owner_column, devices):
    n = owner_row.shape[1]
    same = (owner_column == owner_row) & (iota((n, n), 1) < iota((n, n), 0))
    rank = jnp.sum(jnp.where(same, 1, 0), axis=1, keepdims=True)
    return rank * devices + owner_column


def spread(
    devices, per_owner, points_ref, stiffness_ref, links_ref, owners_ref, slots_ref, loaded_ref,
    out_ref, table_ref, contrib_ref, stage_ref, wait_block,
):
    blocks, k, points, patch = loaded_ref.shape
    parts = []
    for c in range(3):
        rest = points_ref[c]
        for _ in range(3):
            part = rest.astype(BF16).astype(F32)
            parts.append(part)
            rest = rest - part
    parts.append(jnp.zeros_like(parts[0]))
    parts = jnp.concatenate(parts, axis=0).astype(BF16)
    partner = lax.rem(iota(links_ref.shape, 1) + links_ref[...], points)
    diagonal = iota((k, k * points), 0) == iota((k, k * points), 1) // points
    lefts = []
    for b in range(blocks):
        moving = one_hot(iota((points, points), 0) == partner[b:b + 1])
        there = jnp.dot(parts, moving, preferred_element_type=F32)
        rows = []
        for c in range(3):
            r = 3 * c * blocks + b
            found = there[r:r + 1] + there[r + blocks:r + blocks + 1]
            found = found + there[r + 2 * blocks:r + 2 * blocks + 1]
            row = stiffness_ref[b] * (found - points_ref[c, b:b + 1, :])
            rows.append(jnp.where(diagonal, jnp.concatenate([row] * k, axis=1), 0.0))
        rows.append(jnp.zeros_like(rows[0]))
        lefts.append(jnp.concatenate(rows, axis=0).astype(BF16))

    owner_row = to_row(owners_ref[:, 0, :])
    places = slot_row(owner_row, to_column(owner_row), devices)
    total = devices * per_owner
    chosen = iota((total, places.shape[1]), 0) == places
    selector = one_hot(chosen)

    for b in range(blocks):
        wait_block(b)
        right = loaded_ref[b].reshape(k * points, patch)
        result = jnp.dot(lefts[b], right, preferred_element_type=F32)
        for c in range(3):
            contrib_ref[c, b * k:(b + 1) * k, :] = result[c * k:(c + 1) * k]

    tiles = patch // LANES
    width = 3 * tiles * per_owner
    for c in range(3):
        packed = jnp.dot(selector, contrib_ref[c].astype(BF16), preferred_element_type=F32)
        for p in range(per_owner):
            for t in range(tiles):
                stage_ref[pl.ds(p * 3 * tiles + c * tiles + t, devices, stride=width), :] = (
                    packed[p * devices:(p + 1) * devices, t * LANES:(t + 1) * LANES]
                )
    out_ref[...] = stage_ref[...].reshape(out_ref.shape).astype(BF16)
    column = jnp.max(jnp.where(chosen, to_row(slots_ref[...]), -1), axis=1, keepdims=True)
    lane = iota((devices, LANES), 1)
    table = jnp.full((devices, LANES), -1, I32)
    for p in range(per_owner):
        table = jnp.where(lane == p, column[p * devices:(p + 1) * devices], table)
    for d in range(devices):
        table_ref[d] = table[d:d + 1]


HBM = pl.BlockSpec(memory_space=pltpu.HBM)


def each_peer(rows_grid, columns_grid, visit, carry=0):
    gx, gy = lax.axis_index("gx"), lax.axis_index("gy")
    ys = [lax.rem(gy + dy, columns_grid) for dy in range(columns_grid)]
    for dy in range(1, columns_grid):
        visit(dy, (gx, ys[dy]))

    def row(dx, carry):
        x = lax.rem(gx + dx, rows_grid)
        for dy in range(columns_grid):
            visit(dx * columns_grid + dy, (x, ys[dy]))
        return carry

    lax.fori_loop(1, rows_grid, row, 0)


def start_swap(rows_grid, columns_grid, source, target, send_sem, recv_sem):
    devices = rows_grid * columns_grid
    me = lax.axis_index("gx") * columns_grid + lax.axis_index("gy")

    def start(off, to):
        pltpu.make_async_remote_copy(
            src_ref=source.at[to[0] * columns_grid + to[1]], dst_ref=target.at[me],
            send_sem=send_sem, recv_sem=recv_sem, device_id=to, device_id_type=MESH,
        ).start()

    each_peer(rows_grid, columns_grid, start)
    pltpu.make_async_copy(source.at[me], target.at[me], recv_sem).start()

    def wait():
        sent = pl.ds(0, devices - 1)
        pltpu.make_async_copy(source, target, recv_sem).wait()
        pltpu.make_async_copy(source.at[sent], target.at[sent], send_sem).wait()

    return wait


def unpack(stage_ref, devices, per_owner, tiles, c):
    width = 3 * tiles * per_owner
    rows = []
    for p in range(per_owner):
        rows.append(jnp.concatenate(
            [stage_ref[pl.ds(p * 3 * tiles + c * tiles + t, devices, stride=width), :]
             for t in range(tiles)], axis=1))
    return jnp.concatenate(rows, axis=0)


def table_row(table_ref, devices, per_owner):
    total = devices * per_owner
    row = jnp.zeros((1, total), I32)
    for p in range(per_owner):
        column = table_ref[:, 0, :][:, p:p + 1]
        spot = iota((devices, total), 1) == p * devices + iota((devices, total), 0)
        row = row + jnp.sum(jnp.where(spot, column, 0), axis=0, keepdims=True)
    return row


def table_column(table_ref, per_owner):
    return jnp.concatenate([table_ref[:, 0, :][:, p:p + 1] for p in range(per_owner)], axis=0)


def one_hot(mask):
    return mask.astype(F32).astype(BF16)


PAD = 8
UNROLL = 4
assert viscosity == transport_rate
keep = 1.0 - 6.0 * viscosity


def sweep(mid, east, west, north, south, above, below):
    coefficients = [(1 - m, 1 + m) for m in mid]
    out = []
    for c in range(3):
        pairs = [
            ahead * front[c] + behind * back[c]
            for (ahead, behind), (front, back) in zip(
                coefficients, ((east, west), (north, south), (above, below)))
        ]
        out.append(pairs[0] + (pairs[1] + pairs[2]))
    return out


def step_kernel(
    rows_grid, columns_grid, per_owner, points_in, stiffness_in, links_in, owners_in,
    slots_in, weights_ref, velocity_ref,
    fluid_ref, loaded_ref, returned_ref, partial_ref,
    points_ref, stiffness_ref, links_ref, owners_ref, slots_ref, small_sem, received_ref, table_ref, out_ref, outtable_ref, replies_ref, contrib_ref, stage_ref,
    force_ref, first_ref, second_ref, first_half, second_half, taking_ref, sides_send, sides_recv, ends_send, ends_recv,
    halo_ref, send_sem, recv_sem, load_sem, block_sem,
    hsend_sem, hrecv_sem,
):
    devices = rows_grid * columns_grid
    total = devices * per_owner
    tiles, _, layers, rows, _ = fluid_ref.shape
    blocks = weights_ref.shape[0]
    groups = rows // 8
    order = [*range(1, groups - 1), groups - 1, 0]
    pairs = [tuple(order[n:n + 2]) for n in range(0, groups, 2)]
    stride = first_ref.shape[3]
    flat_shape = (3, tiles, layers * stride, LANES)

    def block(b):
        return pltpu.make_async_copy(weights_ref.at[b], loaded_ref.at[b], block_sem.at[b])

    def load(t):
        return pltpu.make_async_copy(
            velocity_ref.at[:, :, :, pl.ds(t * LANES, LANES)], fluid_ref.at[t], load_sem.at[t])

    small = [
        pltpu.make_async_copy(source, target, small_sem.at[n])
        for n, (source, target) in enumerate((
            (points_in, points_ref), (stiffness_in, stiffness_ref), (links_in, links_ref),
            (owners_in, owners_ref), (slots_in, slots_ref)))
    ]
    for copy in small:
        copy.start()
    for b in range(blocks):
        block(b).start(priority=1)

    def wait_block(b):
        block(b).wait()
        if b == blocks - 1:
            for t in range(tiles):
                load(t).start()

    gx, gy = lax.axis_index("gx"), lax.axis_index("gy")
    barrier = pltpu.get_barrier_semaphore()

    def hello(off, to):
        pl.semaphore_signal(barrier, inc=1, device_id=to, device_id_type=MESH)

    each_peer(rows_grid, columns_grid, hello)
    for copy in small:
        copy.wait()
    spread(
        devices, per_owner, points_ref, stiffness_ref, links_ref, owners_ref, slots_ref,
        loaded_ref, out_ref, outtable_ref, contrib_ref, stage_ref, wait_block)
    pl.semaphore_wait(barrier, devices - 1)
    wait_table = start_swap(
        rows_grid, columns_grid, outtable_ref, table_ref, send_sem.at[0], recv_sem.at[0])
    wait = start_swap(
        rows_grid, columns_grid, out_ref, received_ref, send_sem.at[1], recv_sem.at[1])
    for t in range(tiles):
        load(t).wait()
    wait_table()
    wait()

    stage_ref[...] = received_ref[...].astype(F32).reshape(stage_ref.shape)
    for c in range(3):
        force_ref[c] = (force_step * unpack(stage_ref, devices, per_owner, tiles, c)).astype(BF16)
    slots_row = table_row(table_ref, devices, per_owner)
    chunk = 8
    cells = chunk * rows
    lane = iota((16, LANES), 1)
    at_first, at_last = lane == 0, lane == LANES - 1

    unit = one_hot(at_first)

    def gather_end(side, mark, j, value, total_so_far):
        shift = j if side == 0 else lax.rem(j + 1, LANES)
        return total_so_far + mark * pltpu.roll(value, shift, 1)

    zero = jnp.zeros((16, LANES), BF16)

    def settle(n, ends):
        ends = list(ends)
        placing = one_hot(iota((cells, total), 0) + n * cells == slots_row)
        for c in range(3):
            push = jnp.dot(placing, force_ref[c], preferred_element_type=F32)
            for k in range(chunk):
                z = n * chunk + k
                for t in range(tiles):
                    value = fluid_ref[t, c, z] + push[
                        k * rows:(k + 1) * rows, t * LANES:(t + 1) * LANES]
                    first_ref[c, t, z, PAD:PAD + rows, :] = value
                    for n_pair, pair in enumerate(pairs):
                        packed = jnp.concatenate(
                            [value[8 * g:8 * g + 8] for g in pair], axis=0).astype(BF16)
                        first_half[c, t, z, 16 * n_pair:16 * n_pair + 16, :] = packed
                        for side in range(2):
                            if t == side * (tiles - 1):
                                n_end = side * 3 + c
                                j = z * len(pairs) + n_pair
                                ends[n_end] = gather_end(
                                    side, pltpu.roll(unit, j, 1), j, packed, ends[n_end])
        return tuple(ends)

    has = [gx > 0, gx < rows_grid - 1, gy > 0, gy < columns_grid - 1]

    def copies_of(step, wanted=range(4)):
        plan = [
            (sides_send.at[step, 0], sides_recv.at[step, 1], (-1, 0), has[0], has[1]),
            (sides_send.at[step, 1], sides_recv.at[step, 0], (1, 0), has[1], has[0]),
            (ends_send.at[step, 0], ends_recv.at[step, 1], (0, -1), has[2], has[3]),
            (ends_send.at[step, 1], ends_recv.at[step, 0], (0, 1), has[3], has[2]),
        ]
        out = []
        for n, (source, target, (dx, dy), sends, receives) in enumerate(plan):
            if n not in wanted:
                continue
            to = (lax.rem(gx + dx + rows_grid, rows_grid),
                  lax.rem(gy + dy + columns_grid, columns_grid))
            out.append((pltpu.make_async_remote_copy(
                src_ref=source, dst_ref=target, send_sem=hsend_sem.at[step, n],
                recv_sem=hrecv_sem.at[step, n], device_id=to, device_id_type=MESH),
                sends, receives))
        return out

    def send(step, wanted):
        for copy, sends, _ in copies_of(step, wanted):
            @pl.when(sends)
            def _():
                copy.start()

    def send_sides(step, ref):
        flat = ref.reshape(flat_shape)
        for side in range(2):
            row = PAD + side * (rows - 1)
            for c in range(3):
                for t in range(tiles):
                    sides_send[step, side, c, t] = jnp.concatenate(
                        [flat[c, t, pl.ds(g * stride + row, 8, stride=stride), :]
                         for g in range(0, layers, 8)], axis=0).astype(BF16)
        send(step, (0, 1))

    def send_ends(step, ends):
        for side in range(2):
            for c in range(3):
                ends_send[step, side, c] = ends[side * 3 + c]
        send(step, (2, 3))

    def wait_ends(step):
        for copy, _, receives in copies_of(step, (2, 3)):
            @pl.when(receives)
            def _():
                copy.wait_recv()
        for side in range(2):
            for c in range(3):
                halo_ref[side, c] = jnp.where(
                    has[2 + side], ends_recv[step, side, c].astype(F32), 0.0).astype(BF16)

    def wait_sides(step, ref):
        flat = ref.reshape(flat_shape)
        for copy, _, receives in copies_of(step, (0, 1)):
            @pl.when(receives)
            def _():
                copy.wait_recv()
        for side in range(2):
            row = PAD - 1 if side == 0 else PAD + rows
            for c in range(3):
                for t in range(tiles):
                    value = jnp.where(has[side], sides_recv[step, side, c, t].astype(F32), 0.0)
                    for g in range(0, layers, 8):
                        flat[c, t, pl.ds(g * stride + row, 8, stride=stride), :] = value[g:g + 8]

    def sweep_tiles(ref, half, z, k, wanted):
        up, down = lax.rem(z + 1, layers), lax.rem(z + layers - 1, layers)
        j = z * len(pairs) + k
        at = slice(16 * k, 16 * k + 16)

        def beside(c, t, offset):
            return jnp.concatenate(
                [ref[c, t, z, PAD + 8 * g + offset:PAD + 8 * g + offset + 8, :]
                 for g in pairs[k]], axis=0)

        whole, mids = {}, {}

        def mid(c, t):
            if (c, t) not in mids:
                whole[c, t] = beside(c, t, 0)
                mids[c, t] = whole[c, t].astype(BF16)
            return mids[c, t]

        def north(c, t):
            if t == tiles - 1:
                after = pltpu.roll(halo_ref[1, c], lax.rem(LANES - j, LANES), 1)
            else:
                after = mid(c, t + 1)
            return pltpu.roll(jnp.where(at_first, after, mid(c, t)), LANES - 1, 1)

        def south(c, t):
            if t == 0:
                before = pltpu.roll(halo_ref[0, c], LANES - 1 - j, 1)
            else:
                before = mid(c, t - 1)
            return pltpu.roll(jnp.where(at_last, before, mid(c, t)), 1, 1)

        for t in wanted:
            parts = []
            for c in range(3):
                parts.append((
                    mid(c, t), beside(c, t, 1).astype(BF16), beside(c, t, -1).astype(BF16),
                    north(c, t), south(c, t),
                    half[c, t, up, at, :], half[c, t, down, at, :]))
            change = sweep(*[list(v) for v in zip(*parts)])
            yield t, [keep * whole[c, t] + transport_rate * change[c].astype(F32)
                      for c in range(3)]

    def run(ref, half, store, groups_wanted, tiles_wanted, ends=()):
        edge = len(ends) > 0
        unroll = max(1, min(layers, 4 * UNROLL // (len(groups_wanted) * len(tiles_wanted))))

        def body(i, ends):
            ends = list(ends)
            for m in range(unroll):
                z = i * unroll + m
                for k in groups_wanted:
                    j = z * len(pairs) + k
                    mark = pltpu.roll(unit, j, 1)
                    for t, new in sweep_tiles(ref, half, z, k, tiles_wanted):
                        for c in range(3):
                            packed = store(c, t, z, k, new[c])
                            if edge and t in (0, tiles - 1):
                                n_end = (0 if t == 0 else 3) + c
                                ends[n_end] = gather_end(t > 0, mark, j, packed, ends[n_end])
            return tuple(ends)

        return lax.fori_loop(0, layers // unroll, body, ends)

    inner, outer = tuple(range(len(pairs) - 1)), (len(pairs) - 1,)
    middle, border = tuple(range(1, tiles - 1)), (0, tiles - 1)
    half_tiles = tiles // 2
    ends = lax.fori_loop(0, layers // chunk, settle, (zero,) * 6)
    send_ends(0, ends)
    send_sides(0, first_ref)
    slots = table_column(table_ref, per_owner)
    taking_ref[...] = one_hot(iota((total, layers * rows), 1) == slots)

    def store_first(c, t, z, k, value):
        for m, g in enumerate(pairs[k]):
            second_ref[c, t, z, PAD + 8 * g:PAD + 8 * g + 8, :] = value[8 * m:8 * m + 8]
        packed = value.astype(BF16)
        second_half[c, t, z, 16 * k:16 * k + 16, :] = packed
        return packed

    step_one = functools.partial(run, first_ref, first_half, store_first)
    step_one(inner, middle)
    wait_ends(0)
    wait_sides(0, first_ref)
    ends = step_one(outer, border, (zero,) * 6)
    step_one(outer, middle)
    send_sides(1, second_ref)
    ends = step_one(inner, border, ends)
    send_ends(1, ends)

    def store_second(c, t, z, k, value):
        for m, g in enumerate(pairs[k]):
            fluid_ref[t, c, z, 8 * g:8 * g + 8, :] = value[8 * m:8 * m + 8]

    step_two = functools.partial(run, second_ref, second_half, store_second)
    wide = replies_ref.shape[2]
    waits = []
    step_two(inner, middle)
    wait_sides(1, second_ref)
    for h in range(2):
        mine = range(h * half_tiles, (h + 1) * half_tiles)
        step_two(outer, tuple(t for t in mine if t in middle))
        if h == 0:
            wait_ends(1)
        step_two(inner + outer, tuple(t for t in mine if t not in middle))
        for c in range(3):
            flat = jnp.concatenate(
                [fluid_ref[t, c].reshape(layers * rows, LANES).astype(BF16) for t in mine], axis=1)
            part = jnp.dot(taking_ref[...], flat, preferred_element_type=F32)
            for p in range(per_owner):
                for n in range(half_tiles):
                    row = (p * 3 + c) * half_tiles + n
                    stage_ref[pl.ds(row, devices, stride=wide), :] = (
                        part[p * devices:(p + 1) * devices, n * LANES:(n + 1) * LANES])
        replies_ref[h] = stage_ref[0:devices * wide, :].reshape(replies_ref.shape[1:]).astype(BF16)
        waits.append(start_swap(
            rows_grid, columns_grid, replies_ref.at[h], returned_ref.at[h],
            send_sem.at[2 + h], recv_sem.at[2 + h]))
    for step in range(STEPS):
        for copy, sends, _ in copies_of(step):
            @pl.when(sends)
            def _():
                copy.wait_send()
    owner_row = to_row(owners_ref[:, 0, :])
    places = slot_column(owner_row, to_column(owner_row), devices)
    selector = one_hot(iota((places.shape[0], total), 1) == places)
    waits[0]()

    def emit(c, b, value):
        partial_ref[c, b:b + 1, :] = value

    interpolate(0, devices, per_owner, returned_ref, loaded_ref, selector, stage_ref, emit)
    waits[1]()


def interpolate(h, devices, per_owner, returned_ref, loaded_ref, selector, stage_ref, emit):
    blocks, k, points, patch = loaded_ref.shape
    half_tiles = patch // LANES // 2
    wide = returned_ref.shape[2]
    stage_ref[0:devices * wide, :] = returned_ref[h].astype(F32).reshape(devices * wide, LANES)
    picked = []
    for c in range(3):
        replies = jnp.concatenate(
            [jnp.concatenate(
                [stage_ref[pl.ds((p * 3 + c) * half_tiles + n, devices, stride=wide), :]
                 for n in range(half_tiles)], axis=1)
             for p in range(per_owner)], axis=0).astype(BF16)
        picked.append(jnp.dot(selector, replies, preferred_element_type=F32))
    diagonal = iota((k, k * points), 0) == iota((k, k * points), 1) // points
    span = half_tiles * LANES
    for b in range(blocks):
        rows = [picked[c][b * k:(b + 1) * k, :] for c in range(3)]
        rows.append(jnp.zeros_like(rows[0]))
        left = jnp.concatenate(rows, axis=0).astype(BF16)
        right = loaded_ref[b, :, :, h * span:(h + 1) * span].reshape(k * points, span)
        result = lax.dot_general(
            left, right, (((1,), (1,)), ((), ())), preferred_element_type=F32)
        for c in range(3):
            own = jnp.where(diagonal, result[c * k:(c + 1) * k], 0.0)
            fold = own[:, 0:points]
            for n in range(1, k):
                fold = fold + own[:, n * points:(n + 1) * points]
            emit(c, b, jnp.sum(fold, axis=0, keepdims=True))


def finish_kernel(
    devices, per_owner, fluid_ref, loaded_ref, returned_ref, partial_ref, owners_in, points_in,
    out_ref, moved_ref, owners_ref, points_ref, stage_ref, small_sem, store_sem,
):
    def store(t):
        return pltpu.make_async_copy(
            fluid_ref.at[t], out_ref.at[:, :, :, pl.ds(t * LANES, LANES)], store_sem.at[t])

    small = [
        pltpu.make_async_copy(owners_in, owners_ref, small_sem.at[0]),
        pltpu.make_async_copy(points_in, points_ref, small_sem.at[1]),
    ]
    for copy in small:
        copy.start()
    for t in range(fluid_ref.shape[0]):
        store(t).start()
    for copy in small:
        copy.wait()
    owner_row = to_row(owners_ref[:, 0, :])
    places = slot_column(owner_row, to_column(owner_row), devices)
    selector = one_hot(iota((places.shape[0], devices * per_owner), 1) == places)

    def emit(c, b, value):
        moved_ref[c, b:b + 1, :] = points_ref[c, b:b + 1, :] + fiber_step * (
            partial_ref[c, b:b + 1, :] + value)

    interpolate(1, devices, per_owner, returned_ref, loaded_ref, selector, stage_ref, emit)
    for t in range(fluid_ref.shape[0]):
        store(t).wait()


def shards(rows_grid, columns_grid, velocity, fiber_points, stiffness, links, delta_weights,
           owners, patch_slots):
    blocks, intersection, points, patch = delta_weights.shape
    _, layers, rows, columns = velocity.shape
    devices = rows_grid * columns_grid
    entries = blocks * intersection
    per_owner = max(2, (2 * entries + devices - 1) // devices)
    total = devices * per_owner
    tiles = patch // LANES
    width = 3 * tiles * per_owner
    owners = jnp.transpose(owners, (0, 2, 1))
    points_first = jnp.transpose(fiber_points, (1, 0, 2))
    message = jax.ShapeDtypeStruct((devices, width, LANES), BF16)
    wide = -(-3 * (tiles // 2) * per_owner // 8) * 8
    reply = jax.ShapeDtypeStruct((2, devices, wide, LANES), BF16)
    table_shape = jax.ShapeDtypeStruct((devices, 1, LANES), I32)
    stage = pltpu.VMEM((devices * max(width, wide), LANES), F32)
    limit = 32 << 20
    field = pltpu.VMEM((3, tiles, layers, rows + 2 * PAD, LANES), F32)
    half = pltpu.VMEM((3, tiles, layers, rows, LANES), BF16)
    sides = pltpu.VMEM((STEPS, 2, 3, tiles, layers, LANES), BF16)
    ends = pltpu.VMEM((STEPS, 2, 3, 16, LANES), BF16)
    fluid_tiles, weights, returned, partial = pl.pallas_call(
        functools.partial(step_kernel, rows_grid, columns_grid, per_owner),
        out_shape=[
            jax.ShapeDtypeStruct((tiles, 3, layers, rows, LANES), F32),
            jax.ShapeDtypeStruct(delta_weights.shape, BF16),
            reply,
            jax.ShapeDtypeStruct(points_first.shape, F32),
        ],
        in_specs=[HBM] * 7,
        out_specs=[VMEM] * 4,
        scratch_shapes=[
            pltpu.VMEM(points_first.shape, F32),
            pltpu.SMEM(stiffness.shape, F32),
            pltpu.VMEM(links.shape, I32),
            pltpu.VMEM(owners.shape, I32),
            pltpu.VMEM(patch_slots.shape, I32),
            pltpu.SemaphoreType.DMA((5,)),
            pltpu.VMEM(message.shape, BF16),
            pltpu.VMEM(table_shape.shape, I32),
            pltpu.VMEM(message.shape, BF16),
            pltpu.VMEM(table_shape.shape, I32),
            pltpu.VMEM(reply.shape, BF16),
            pltpu.VMEM((3, entries, patch), F32),
            stage,
            pltpu.VMEM((3, total, patch), BF16),
            field, field, half, half,
            pltpu.VMEM((total, layers * rows), BF16),
            sides, sides, ends, ends,
            pltpu.VMEM((2, 3, 16, LANES), BF16),
            pltpu.SemaphoreType.DMA((4,)),
            pltpu.SemaphoreType.DMA((4,)),
            pltpu.SemaphoreType.DMA((tiles,)),
            pltpu.SemaphoreType.DMA((blocks,)),
            pltpu.SemaphoreType.DMA((STEPS, 4)),
            pltpu.SemaphoreType.DMA((STEPS, 4)),
        ],
        compiler_params=pltpu.CompilerParams(
            collective_id=0, has_side_effects=True, vmem_limit_bytes=limit),
    )(*[pltpu.with_memory_space_constraint(v, pltpu.HBM) for v in (
        points_first, stiffness, links, owners, patch_slots, delta_weights, velocity)])

    fluid, moved = pl.pallas_call(
        functools.partial(finish_kernel, devices, per_owner),
        out_shape=[
            jax.ShapeDtypeStruct(velocity.shape, F32),
            jax.ShapeDtypeStruct(points_first.shape, F32),
        ],
        in_specs=[VMEM, VMEM, VMEM, VMEM, HBM, HBM],
        out_specs=[HBM, VMEM],
        scratch_shapes=[
            pltpu.VMEM(owners.shape, I32),
            pltpu.VMEM(points_first.shape, F32),
            stage,
            pltpu.SemaphoreType.DMA((2,)),
            pltpu.SemaphoreType.DMA((tiles,)),
        ],
        compiler_params=pltpu.CompilerParams(vmem_limit_bytes=8 << 20),
    )(fluid_tiles, weights, returned, partial, pltpu.with_memory_space_constraint(owners, pltpu.HBM),
      pltpu.with_memory_space_constraint(points_first, pltpu.HBM))
    return fluid, jnp.transpose(moved, (1, 0, 2))


def solution(mesh):
    placed = (
        P(None, None, "gx", "gy"),
        P(("gx", "gy"), None, None),
        P(("gx", "gy")),
        P(("gx", "gy"), None),
        P(("gx", "gy"), None, None, None),
        P(("gx", "gy"), None, None),
        P(("gx", "gy"), None),
    )
    return jax.shard_map(
        functools.partial(shards, mesh.shape["gx"], mesh.shape["gy"]),
        mesh=mesh,
        in_specs=placed,
        out_specs=(placed[0], placed[1]),
        check_vma=False,
    )
```

```python
import functools

import jax
import jax.numpy as jnp
from jax import lax
from jax.experimental import pallas as pl
from jax.experimental.pallas import tpu as pltpu
from jax.sharding import PartitionSpec as P

STEPS = 2
viscosity = 0.1
transport_rate = 0.1
force_step = 0.5
fiber_step = 0.25

F32 = jnp.float32
BF16 = jnp.bfloat16
I32 = jnp.int32
LANES = 128
MESH = pl.DeviceIdType.MESH
VMEM = pl.BlockSpec(memory_space=pltpu.VMEM)
ANY = pl.BlockSpec(memory_space=pl.ANY)
SMEM = pl.BlockSpec(memory_space=pltpu.SMEM)


def iota(shape, dim):
    return lax.broadcasted_iota(I32, shape, dim)


def to_column(row):
    n = row.shape[1]
    return jnp.sum(jnp.where(iota((n, n), 0) == iota((n, n), 1), row, 0), axis=1, keepdims=True)


def to_row(grid):
    n, k = grid.shape
    tiled = jnp.concatenate([grid] * n, axis=1)
    return jnp.sum(
        jnp.where(iota((n, n * k), 0) == iota((n, n * k), 1) // k, tiled, 0), axis=0, keepdims=True)


def slot_row(owner_row, owner_column, devices):
    n = owner_row.shape[1]
    same = (owner_column == owner_row) & (iota((n, n), 0) < iota((n, n), 1))
    rank = jnp.sum(jnp.where(same, 1, 0), axis=0, keepdims=True)
    return rank * devices + owner_row


def slot_column(owner_row, owner_column, devices):
    n = owner_row.shape[1]
    same = (owner_column == owner_row) & (iota((n, n), 1) < iota((n, n), 0))
    rank = jnp.sum(jnp.where(same, 1, 0), axis=1, keepdims=True)
    return rank * devices + owner_column


def spread(
    devices, per_owner, points_ref, stiffness_ref, links_ref, owners_ref, slots_ref, loaded_ref,
    out_ref, table_ref, contrib_ref, stage_ref, wait_block,
):
    blocks, k, points, patch = loaded_ref.shape
    parts = []
    for c in range(3):
        rest = points_ref[c]
        for _ in range(3):
            part = rest.astype(BF16).astype(F32)
            parts.append(part)
            rest = rest - part
    parts.append(jnp.zeros_like(parts[0]))
    parts = jnp.concatenate(parts, axis=0).astype(BF16)
    partner = lax.rem(iota(links_ref.shape, 1) + links_ref[...], points)
    diagonal = iota((k, k * points), 0) == iota((k, k * points), 1) // points
    lefts = []
    for b in range(blocks):
        moving = one_hot(iota((points, points), 0) == partner[b:b + 1])
        there = jnp.dot(parts, moving, preferred_element_type=F32)
        rows = []
        for c in range(3):
            r = 3 * c * blocks + b
            found = there[r:r + 1] + there[r + blocks:r + blocks + 1]
            found = found + there[r + 2 * blocks:r + 2 * blocks + 1]
            row = stiffness_ref[b] * (found - points_ref[c, b:b + 1, :])
            rows.append(jnp.where(diagonal, jnp.concatenate([row] * k, axis=1), 0.0))
        rows.append(jnp.zeros_like(rows[0]))
        lefts.append(jnp.concatenate(rows, axis=0).astype(BF16))

    owner_row = to_row(owners_ref[:, 0, :])
    places = slot_row(owner_row, to_column(owner_row), devices)
    total = devices * per_owner
    chosen = iota((total, places.shape[1]), 0) == places
    selector = one_hot(chosen)

    for b in range(blocks):
        wait_block(b)
        right = loaded_ref[b].reshape(k * points, patch)
        result = jnp.dot(lefts[b], right, preferred_element_type=F32)
        for c in range(3):
            contrib_ref[c, b * k:(b + 1) * k, :] = result[c * k:(c + 1) * k]

    tiles = patch // LANES
    width = 3 * tiles * per_owner
    for c in range(3):
        packed = jnp.dot(selector, contrib_ref[c].astype(BF16), preferred_element_type=F32)
        for p in range(per_owner):
            for t in range(tiles):
                stage_ref[pl.ds(p * 3 * tiles + c * tiles + t, devices, stride=width), :] = (
                    packed[p * devices:(p + 1) * devices, t * LANES:(t + 1) * LANES]
                )
    out_ref[...] = stage_ref[...].reshape(out_ref.shape).astype(BF16)
    column = jnp.max(jnp.where(chosen, to_row(slots_ref[...]), -1), axis=1, keepdims=True)
    lane = iota((devices, LANES), 1)
    table = jnp.full((devices, LANES), -1, I32)
    for p in range(per_owner):
        table = jnp.where(lane == p, column[p * devices:(p + 1) * devices], table)
    for d in range(devices):
        table_ref[d] = table[d:d + 1]


HBM = pl.BlockSpec(memory_space=pltpu.HBM)


def each_peer(rows_grid, columns_grid, visit, carry=0):
    gx, gy = lax.axis_index("gx"), lax.axis_index("gy")
    ys = [lax.rem(gy + dy, columns_grid) for dy in range(columns_grid)]
    for dy in range(1, columns_grid):
        visit(dy, (gx, ys[dy]))

    def row(dx, carry):
        x = lax.rem(gx + dx, rows_grid)
        for dy in range(columns_grid):
            visit(dx * columns_grid + dy, (x, ys[dy]))
        return carry

    lax.fori_loop(1, rows_grid, row, 0)


def start_swap(rows_grid, columns_grid, source, target, send_sem, recv_sem):
    devices = rows_grid * columns_grid
    me = lax.axis_index("gx") * columns_grid + lax.axis_index("gy")

    def start(off, to):
        pltpu.make_async_remote_copy(
            src_ref=source.at[to[0] * columns_grid + to[1]], dst_ref=target.at[me],
            send_sem=send_sem, recv_sem=recv_sem, device_id=to, device_id_type=MESH,
        ).start()

    each_peer(rows_grid, columns_grid, start)
    pltpu.make_async_copy(source.at[me], target.at[me], recv_sem).start()

    def wait():
        sent = pl.ds(0, devices - 1)
        pltpu.make_async_copy(source, target, recv_sem).wait()
        pltpu.make_async_copy(source.at[sent], target.at[sent], send_sem).wait()

    return wait


def unpack(stage_ref, devices, per_owner, tiles, c):
    width = 3 * tiles * per_owner
    rows = []
    for p in range(per_owner):
        rows.append(jnp.concatenate(
            [stage_ref[pl.ds(p * 3 * tiles + c * tiles + t, devices, stride=width), :]
             for t in range(tiles)], axis=1))
    return jnp.concatenate(rows, axis=0)


def table_row(table_ref, devices, per_owner):
    total = devices * per_owner
    row = jnp.zeros((1, total), I32)
    for p in range(per_owner):
        column = table_ref[:, 0, :][:, p:p + 1]
        spot = iota((devices, total), 1) == p * devices + iota((devices, total), 0)
        row = row + jnp.sum(jnp.where(spot, column, 0), axis=0, keepdims=True)
    return row


def table_column(table_ref, per_owner):
    return jnp.concatenate([table_ref[:, 0, :][:, p:p + 1] for p in range(per_owner)], axis=0)


def one_hot(mask):
    return mask.astype(F32).astype(BF16)


PAD = 8
UNROLL = 4
assert viscosity == transport_rate
keep = 1.0 - 6.0 * viscosity


def sweep(mid, east, west, north, south, above, below):
    coefficients = [(1 - m, 1 + m) for m in mid]
    out = []
    for c in range(3):
        pairs = [
            ahead * front[c] + behind * back[c]
            for (ahead, behind), (front, back) in zip(
                coefficients, ((east, west), (north, south), (above, below)))
        ]
        out.append(pairs[0] + (pairs[1] + pairs[2]))
    return out


def step_kernel(
    rows_grid, columns_grid, per_owner, points_in, stiffness_in, links_in, owners_in,
    slots_in, weights_ref, velocity_ref,
    fluid_ref, loaded_ref, returned_ref, partial_ref,
    points_ref, stiffness_ref, links_ref, owners_ref, slots_ref, small_sem, received_ref, table_ref, out_ref, outtable_ref, replies_ref, contrib_ref, stage_ref,
    force_ref, first_ref, second_ref, first_half, second_half, taking_ref, sides_send, sides_recv, ends_send, ends_recv,
    halo_ref, send_sem, recv_sem, load_sem, block_sem,
    hsend_sem, hrecv_sem,
):
    devices = rows_grid * columns_grid
    total = devices * per_owner
    tiles, _, layers, rows, _ = fluid_ref.shape
    blocks = weights_ref.shape[0]
    groups = rows // 8
    order = [*range(1, groups - 1), groups - 1, 0]
    pairs = [tuple(order[n:n + 2]) for n in range(0, groups, 2)]
    stride = first_ref.shape[3]
    flat_shape = (3, tiles, layers * stride, LANES)

    def block(b):
        return pltpu.make_async_copy(weights_ref.at[b], loaded_ref.at[b], block_sem.at[b])

    def load(t):
        return pltpu.make_async_copy(
            velocity_ref.at[:, :, :, pl.ds(t * LANES, LANES)], fluid_ref.at[t], load_sem.at[t])

    small = [
        pltpu.make_async_copy(source, target, small_sem.at[n])
        for n, (source, target) in enumerate((
            (points_in, points_ref), (stiffness_in, stiffness_ref), (links_in, links_ref),
            (owners_in, owners_ref), (slots_in, slots_ref)))
    ]
    for copy in small:
        copy.start()
    for b in range(blocks):
        block(b).start(priority=1)

    def wait_block(b):
        block(b).wait()
        if b == blocks - 1:
            for t in range(tiles):
                load(t).start()

    gx, gy = lax.axis_index("gx"), lax.axis_index("gy")
    barrier = pltpu.get_barrier_semaphore()

    def hello(off, to):
        pl.semaphore_signal(barrier, inc=1, device_id=to, device_id_type=MESH)

    each_peer(rows_grid, columns_grid, hello)
    for copy in small:
        copy.wait()
    spread(
        devices, per_owner, points_ref, stiffness_ref, links_ref, owners_ref, slots_ref,
        loaded_ref, out_ref, outtable_ref, contrib_ref, stage_ref, wait_block)
    pl.semaphore_wait(barrier, devices - 1)
    wait_table = start_swap(
        rows_grid, columns_grid, outtable_ref, table_ref, send_sem.at[0], recv_sem.at[0])
    wait = start_swap(
        rows_grid, columns_grid, out_ref, received_ref, send_sem.at[1], recv_sem.at[1])
    for t in range(tiles):
        load(t).wait()
    wait_table()
    wait()

    stage_ref[...] = received_ref[...].astype(F32).reshape(stage_ref.shape)
    for c in range(3):
        force_ref[c] = (force_step * unpack(stage_ref, devices, per_owner, tiles, c)).astype(BF16)
    slots_row = table_row(table_ref, devices, per_owner)
    chunk = 8
    cells = chunk * rows
    lane = iota((16, LANES), 1)
    at_first, at_last = lane == 0, lane == LANES - 1

    unit = one_hot(at_first | at_last)

    def edge_lane(z, k):
        return 2 * (z * len(pairs) + k) + 1

    def gather_end(j, mark, low, high, total_so_far):
        return total_so_far + mark * pltpu.roll(jnp.where(at_first, low, high), j, 1)

    zero = jnp.zeros((16, LANES), BF16)

    def settle(n, ends):
        ends = list(ends)
        placing = one_hot(iota((cells, total), 0) + n * cells == slots_row)
        marks = {
            (k, n_pair): pltpu.roll(unit, edge_lane(n * chunk + k, n_pair), 1)
            for k in range(chunk) for n_pair in range(len(pairs))
        }
        for c in range(3):
            push = jnp.dot(placing, force_ref[c], preferred_element_type=F32)
            for k in range(chunk):
                z = n * chunk + k
                edges = {}
                for t in range(tiles):
                    value = fluid_ref[t, c, z] + push[
                        k * rows:(k + 1) * rows, t * LANES:(t + 1) * LANES]
                    first_ref[c, t, z, PAD:PAD + rows, :] = value
                    for n_pair, pair in enumerate(pairs):
                        packed = jnp.concatenate(
                            [value[8 * g:8 * g + 8] for g in pair], axis=0).astype(BF16)
                        first_half[c, t, z, 16 * n_pair:16 * n_pair + 16, :] = packed
                        edges[t, n_pair] = packed
                for n_pair in range(len(pairs)):
                    ends[c] = gather_end(
                        edge_lane(z, n_pair), marks[k, n_pair], edges[0, n_pair],
                        edges[tiles - 1, n_pair], ends[c])
        return tuple(ends)

    has = [gx > 0, gx < rows_grid - 1, gy > 0, gy < columns_grid - 1]

    def copies_of(step, wanted=range(4)):
        plan = [
            (sides_send.at[step, 0], sides_recv.at[step, 1], (-1, 0), has[0], has[1]),
            (sides_send.at[step, 1], sides_recv.at[step, 0], (1, 0), has[1], has[0]),
            (ends_send.at[step], ends_recv.at[step, 1], (0, -1), has[2], has[3]),
            (ends_send.at[step], ends_recv.at[step, 0], (0, 1), has[3], has[2]),
        ]
        out = []
        for n, (source, target, (dx, dy), sends, receives) in enumerate(plan):
            if n not in wanted:
                continue
            to = (lax.rem(gx + dx + rows_grid, rows_grid),
                  lax.rem(gy + dy + columns_grid, columns_grid))
            out.append((pltpu.make_async_remote_copy(
                src_ref=source, dst_ref=target, send_sem=hsend_sem.at[step, n],
                recv_sem=hrecv_sem.at[step, n], device_id=to, device_id_type=MESH),
                sends, receives))
        return out

    def send(step, wanted):
        for copy, sends, _ in copies_of(step, wanted):
            @pl.when(sends)
            def _():
                copy.start()

    def send_sides(step, ref):
        flat = ref.reshape(flat_shape)
        for side in range(2):
            row = PAD + side * (rows - 1)
            for c in range(3):
                for t in range(tiles):
                    sides_send[step, side, c, t] = jnp.concatenate(
                        [flat[c, t, pl.ds(g * stride + row, 8, stride=stride), :]
                         for g in range(0, layers, 8)], axis=0).astype(BF16)
        send(step, (0, 1))

    def send_ends(step, ends):
        for c in range(3):
            ends_send[step, c] = ends[c]
        send(step, (2, 3))

    def wait_ends(step):
        for copy, _, receives in copies_of(step, (2, 3)):
            @pl.when(receives)
            def _():
                copy.wait_recv()
        even = lax.rem(lane, 2) == 0
        for c in range(3):
            south, north = [ends_recv[step, side, c].astype(F32) for side in range(2)]
            halo_ref[c] = jnp.where(
                even, jnp.where(has[2], south, 0.0), jnp.where(has[3], north, 0.0)).astype(BF16)

    def wait_sides(step, ref):
        flat = ref.reshape(flat_shape)
        for copy, _, receives in copies_of(step, (0, 1)):
            @pl.when(receives)
            def _():
                copy.wait_recv()
        for side in range(2):
            row = PAD - 1 if side == 0 else PAD + rows
            for c in range(3):
                for t in range(tiles):
                    value = jnp.where(has[side], sides_recv[step, side, c, t].astype(F32), 0.0)
                    for g in range(0, layers, 8):
                        flat[c, t, pl.ds(g * stride + row, 8, stride=stride), :] = value[g:g + 8]

    def sweep_tiles(ref, half, z, k, wanted):
        up, down = lax.rem(z + 1, layers), lax.rem(z + layers - 1, layers)
        j = edge_lane(z, k)
        at = slice(16 * k, 16 * k + 16)

        def beside(c, t, offset):
            return jnp.concatenate(
                [ref[c, t, z, PAD + 8 * g + offset:PAD + 8 * g + offset + 8, :]
                 for g in pairs[k]], axis=0)

        whole, mids = {}, {}

        def mid(c, t):
            if (c, t) not in mids:
                whole[c, t] = beside(c, t, 0)
                mids[c, t] = whole[c, t].astype(BF16)
            return mids[c, t]

        outside = {}

        def beyond(c):
            if c not in outside:
                outside[c] = pltpu.roll(halo_ref[c], LANES - j, 1)
            return outside[c]

        def north(c, t):
            if t == tiles - 1:
                after = beyond(c)
            else:
                after = mid(c, t + 1)
            return pltpu.roll(jnp.where(at_first, after, mid(c, t)), LANES - 1, 1)

        def south(c, t):
            if t == 0:
                before = beyond(c)
            else:
                before = mid(c, t - 1)
            return pltpu.roll(jnp.where(at_last, before, mid(c, t)), 1, 1)

        for t in wanted:
            parts = []
            for c in range(3):
                parts.append((
                    mid(c, t), beside(c, t, 1).astype(BF16), beside(c, t, -1).astype(BF16),
                    north(c, t), south(c, t),
                    half[c, t, up, at, :], half[c, t, down, at, :]))
            change = sweep(*[list(v) for v in zip(*parts)])
            yield t, [keep * whole[c, t] + transport_rate * change[c].astype(F32)
                      for c in range(3)]

    def run(ref, half, store, groups_wanted, tiles_wanted, ends=()):
        edge = len(ends) > 0
        unroll = max(1, min(layers, 4 * UNROLL // (len(groups_wanted) * len(tiles_wanted))))

        def body(i, ends):
            ends = list(ends)
            for m in range(unroll):
                z = i * unroll + m
                for k in groups_wanted:
                    edges = {}
                    for t, new in sweep_tiles(ref, half, z, k, tiles_wanted):
                        for c in range(3):
                            edges[c, t] = store(c, t, z, k, new[c])
                    if edge:
                        j = edge_lane(z, k)
                        mark = pltpu.roll(unit, j, 1)
                        for c in range(3):
                            ends[c] = gather_end(
                                j, mark, edges[c, 0], edges[c, tiles - 1], ends[c])
            return tuple(ends)

        return lax.fori_loop(0, layers // unroll, body, ends)

    inner, outer = tuple(range(len(pairs) - 1)), (len(pairs) - 1,)
    middle, border = tuple(range(1, tiles - 1)), (0, tiles - 1)
    half_tiles = tiles // 2
    ends = lax.fori_loop(0, layers // chunk, settle, (zero,) * 3)
    send_ends(0, ends)
    send_sides(0, first_ref)
    slots = table_column(table_ref, per_owner)
    taking_ref[...] = one_hot(iota((total, layers * rows), 1) == slots)

    def store_first(c, t, z, k, value):
        for m, g in enumerate(pairs[k]):
            second_ref[c, t, z, PAD + 8 * g:PAD + 8 * g + 8, :] = value[8 * m:8 * m + 8]
        packed = value.astype(BF16)
        second_half[c, t, z, 16 * k:16 * k + 16, :] = packed
        return packed

    step_one = functools.partial(run, first_ref, first_half, store_first)
    step_one(inner, middle)
    wait_ends(0)
    ends = step_one(inner, border, (zero,) * 3)
    wait_sides(0, first_ref)
    ends = step_one(outer, border, ends)
    send_ends(1, ends)
    step_one(outer, middle)
    send_sides(1, second_ref)

    def store_second(c, t, z, k, value):
        for m, g in enumerate(pairs[k]):
            fluid_ref[t, c, z, 8 * g:8 * g + 8, :] = value[8 * m:8 * m + 8]

    step_two = functools.partial(run, second_ref, second_half, store_second)
    wide = replies_ref.shape[2]
    waits = []
    step_two(inner, middle)
    wait_ends(1)
    step_two(inner, border)
    wait_sides(1, second_ref)
    for h in range(2):
        mine = tuple(range(h * half_tiles, (h + 1) * half_tiles))
        step_two(outer, mine)
        for c in range(3):
            flat = jnp.concatenate(
                [fluid_ref[t, c].reshape(layers * rows, LANES).astype(BF16) for t in mine], axis=1)
            part = jnp.dot(taking_ref[...], flat, preferred_element_type=F32)
            for p in range(per_owner):
                for n in range(half_tiles):
                    row = (p * 3 + c) * half_tiles + n
                    stage_ref[pl.ds(row, devices, stride=wide), :] = (
                        part[p * devices:(p + 1) * devices, n * LANES:(n + 1) * LANES])
        replies_ref[h] = stage_ref[0:devices * wide, :].reshape(replies_ref.shape[1:]).astype(BF16)
        waits.append(start_swap(
            rows_grid, columns_grid, replies_ref.at[h], returned_ref.at[h],
            send_sem.at[2 + h], recv_sem.at[2 + h]))
    for step in range(STEPS):
        for copy, sends, _ in copies_of(step):
            @pl.when(sends)
            def _():
                copy.wait_send()
    owner_row = to_row(owners_ref[:, 0, :])
    places = slot_column(owner_row, to_column(owner_row), devices)
    selector = one_hot(iota((places.shape[0], total), 1) == places)
    waits[0]()

    def emit(c, b, value):
        partial_ref[c, b:b + 1, :] = value

    interpolate(0, devices, per_owner, returned_ref, loaded_ref, selector, stage_ref, emit)
    waits[1]()


def interpolate(h, devices, per_owner, returned_ref, loaded_ref, selector, stage_ref, emit):
    blocks, k, points, patch = loaded_ref.shape
    half_tiles = patch // LANES // 2
    wide = returned_ref.shape[2]
    stage_ref[0:devices * wide, :] = returned_ref[h].astype(F32).reshape(devices * wide, LANES)
    picked = []
    for c in range(3):
        replies = jnp.concatenate(
            [jnp.concatenate(
                [stage_ref[pl.ds((p * 3 + c) * half_tiles + n, devices, stride=wide), :]
                 for n in range(half_tiles)], axis=1)
             for p in range(per_owner)], axis=0).astype(BF16)
        picked.append(jnp.dot(selector, replies, preferred_element_type=F32))
    diagonal = iota((k, k * points), 0) == iota((k, k * points), 1) // points
    span = half_tiles * LANES
    for b in range(blocks):
        rows = [picked[c][b * k:(b + 1) * k, :] for c in range(3)]
        rows.append(jnp.zeros_like(rows[0]))
        left = jnp.concatenate(rows, axis=0).astype(BF16)
        right = loaded_ref[b, :, :, h * span:(h + 1) * span].reshape(k * points, span)
        result = lax.dot_general(
            left, right, (((1,), (1,)), ((), ())), preferred_element_type=F32)
        for c in range(3):
            own = jnp.where(diagonal, result[c * k:(c + 1) * k], 0.0)
            fold = own[:, 0:points]
            for n in range(1, k):
                fold = fold + own[:, n * points:(n + 1) * points]
            emit(c, b, jnp.sum(fold, axis=0, keepdims=True))


def finish_kernel(
    devices, per_owner, fluid_ref, loaded_ref, returned_ref, partial_ref, owners_in, points_in,
    out_ref, moved_ref, owners_ref, points_ref, stage_ref, small_sem, store_sem,
):
    def store(t):
        return pltpu.make_async_copy(
            fluid_ref.at[t], out_ref.at[:, :, :, pl.ds(t * LANES, LANES)], store_sem.at[t])

    small = [
        pltpu.make_async_copy(owners_in, owners_ref, small_sem.at[0]),
        pltpu.make_async_copy(points_in, points_ref, small_sem.at[1]),
    ]
    for copy in small:
        copy.start()
    for t in range(fluid_ref.shape[0]):
        store(t).start()
    for copy in small:
        copy.wait()
    owner_row = to_row(owners_ref[:, 0, :])
    places = slot_column(owner_row, to_column(owner_row), devices)
    selector = one_hot(iota((places.shape[0], devices * per_owner), 1) == places)

    def emit(c, b, value):
        moved_ref[c, b:b + 1, :] = points_ref[c, b:b + 1, :] + fiber_step * (
            partial_ref[c, b:b + 1, :] + value)

    interpolate(1, devices, per_owner, returned_ref, loaded_ref, selector, stage_ref, emit)
    for t in range(fluid_ref.shape[0]):
        store(t).wait()


def shards(rows_grid, columns_grid, velocity, fiber_points, stiffness, links, delta_weights,
           owners, patch_slots):
    blocks, intersection, points, patch = delta_weights.shape
    _, layers, rows, columns = velocity.shape
    devices = rows_grid * columns_grid
    entries = blocks * intersection
    per_owner = max(2, (2 * entries + devices - 1) // devices)
    total = devices * per_owner
    tiles = patch // LANES
    width = 3 * tiles * per_owner
    owners = jnp.transpose(owners, (0, 2, 1))
    points_first = jnp.transpose(fiber_points, (1, 0, 2))
    message = jax.ShapeDtypeStruct((devices, width, LANES), BF16)
    wide = -(-3 * (tiles // 2) * per_owner // 8) * 8
    reply = jax.ShapeDtypeStruct((2, devices, wide, LANES), BF16)
    table_shape = jax.ShapeDtypeStruct((devices, 1, LANES), I32)
    stage = pltpu.VMEM((devices * max(width, wide), LANES), F32)
    limit = 32 << 20
    field = pltpu.VMEM((3, tiles, layers, rows + 2 * PAD, LANES), F32)
    half = pltpu.VMEM((3, tiles, layers, rows, LANES), BF16)
    sides = pltpu.VMEM((STEPS, 2, 3, tiles, layers, LANES), BF16)
    fluid_tiles, weights, returned, partial = pl.pallas_call(
        functools.partial(step_kernel, rows_grid, columns_grid, per_owner),
        out_shape=[
            jax.ShapeDtypeStruct((tiles, 3, layers, rows, LANES), F32),
            jax.ShapeDtypeStruct(delta_weights.shape, BF16),
            reply,
            jax.ShapeDtypeStruct(points_first.shape, F32),
        ],
        in_specs=[HBM] * 7,
        out_specs=[VMEM] * 4,
        scratch_shapes=[
            pltpu.VMEM(points_first.shape, F32),
            pltpu.SMEM(stiffness.shape, F32),
            pltpu.VMEM(links.shape, I32),
            pltpu.VMEM(owners.shape, I32),
            pltpu.VMEM(patch_slots.shape, I32),
            pltpu.SemaphoreType.DMA((5,)),
            pltpu.VMEM(message.shape, BF16),
            pltpu.VMEM(table_shape.shape, I32),
            pltpu.VMEM(message.shape, BF16),
            pltpu.VMEM(table_shape.shape, I32),
            pltpu.VMEM(reply.shape, BF16),
            pltpu.VMEM((3, entries, patch), F32),
            stage,
            pltpu.VMEM((3, total, patch), BF16),
            field, field, half, half,
            pltpu.VMEM((total, layers * rows), BF16),
            sides, sides,
            pltpu.VMEM((STEPS, 3, 16, LANES), BF16),
            pltpu.VMEM((STEPS, 2, 3, 16, LANES), BF16),
            pltpu.VMEM((3, 16, LANES), BF16),
            pltpu.SemaphoreType.DMA((4,)),
            pltpu.SemaphoreType.DMA((4,)),
            pltpu.SemaphoreType.DMA((tiles,)),
            pltpu.SemaphoreType.DMA((blocks,)),
            pltpu.SemaphoreType.DMA((STEPS, 4)),
            pltpu.SemaphoreType.DMA((STEPS, 4)),
        ],
        compiler_params=pltpu.CompilerParams(
            collective_id=0, has_side_effects=True, vmem_limit_bytes=limit),
    )(*[pltpu.with_memory_space_constraint(v, pltpu.HBM) for v in (
        points_first, stiffness, links, owners, patch_slots, delta_weights, velocity)])

    fluid, moved = pl.pallas_call(
        functools.partial(finish_kernel, devices, per_owner),
        out_shape=[
            jax.ShapeDtypeStruct(velocity.shape, F32),
            jax.ShapeDtypeStruct(points_first.shape, F32),
        ],
        in_specs=[VMEM, VMEM, VMEM, VMEM, HBM, HBM],
        out_specs=[HBM, VMEM],
        scratch_shapes=[
            pltpu.VMEM(owners.shape, I32),
            pltpu.VMEM(points_first.shape, F32),
            stage,
            pltpu.SemaphoreType.DMA((2,)),
            pltpu.SemaphoreType.DMA((tiles,)),
        ],
        compiler_params=pltpu.CompilerParams(vmem_limit_bytes=8 << 20),
    )(fluid_tiles, weights, returned, partial, pltpu.with_memory_space_constraint(owners, pltpu.HBM),
      pltpu.with_memory_space_constraint(points_first, pltpu.HBM))
    return fluid, jnp.transpose(moved, (1, 0, 2))


def solution(mesh):
    placed = (
        P(None, None, "gx", "gy"),
        P(("gx", "gy"), None, None),
        P(("gx", "gy")),
        P(("gx", "gy"), None),
        P(("gx", "gy"), None, None, None),
        P(("gx", "gy"), None, None),
        P(("gx", "gy"), None),
    )
    return jax.shard_map(
        functools.partial(shards, mesh.shape["gx"], mesh.shape["gy"]),
        mesh=mesh,
        in_specs=placed,
        out_specs=(placed[0], placed[1]),
        check_vma=False,
    )
```

```python
import functools

import jax
import jax.numpy as jnp
from jax import lax
from jax.experimental import pallas as pl
from jax.experimental.pallas import tpu as pltpu
from jax.sharding import PartitionSpec as P

STEPS = 2
viscosity = 0.1
transport_rate = 0.1
force_step = 0.5
fiber_step = 0.25

F32 = jnp.float32
BF16 = jnp.bfloat16
I32 = jnp.int32
LANES = 128
MESH = pl.DeviceIdType.MESH
VMEM = pl.BlockSpec(memory_space=pltpu.VMEM)
ANY = pl.BlockSpec(memory_space=pl.ANY)
SMEM = pl.BlockSpec(memory_space=pltpu.SMEM)


def iota(shape, dim):
    return lax.broadcasted_iota(I32, shape, dim)


def to_column(row):
    n = row.shape[1]
    return jnp.sum(jnp.where(iota((n, n), 0) == iota((n, n), 1), row, 0), axis=1, keepdims=True)


def to_row(grid):
    n, k = grid.shape
    tiled = jnp.concatenate([grid] * n, axis=1)
    return jnp.sum(
        jnp.where(iota((n, n * k), 0) == iota((n, n * k), 1) // k, tiled, 0), axis=0, keepdims=True)


def slot_row(owner_row, owner_column, devices):
    n = owner_row.shape[1]
    same = (owner_column == owner_row) & (iota((n, n), 0) < iota((n, n), 1))
    rank = jnp.sum(jnp.where(same, 1, 0), axis=0, keepdims=True)
    return rank * devices + owner_row


def slot_column(owner_row, owner_column, devices):
    n = owner_row.shape[1]
    same = (owner_column == owner_row) & (iota((n, n), 1) < iota((n, n), 0))
    rank = jnp.sum(jnp.where(same, 1, 0), axis=1, keepdims=True)
    return rank * devices + owner_column


def spread(
    devices, per_owner, points_ref, stiffness_ref, links_ref, owners_ref, slots_ref, loaded_ref,
    out_ref, table_ref, contrib_ref, stage_ref, wait_block,
):
    blocks, k, points, patch = loaded_ref.shape
    parts = []
    for c in range(3):
        rest = points_ref[c]
        for _ in range(3):
            part = rest.astype(BF16).astype(F32)
            parts.append(part)
            rest = rest - part
    parts.append(jnp.zeros_like(parts[0]))
    parts = jnp.concatenate(parts, axis=0).astype(BF16)
    partner = lax.rem(iota(links_ref.shape, 1) + links_ref[...], points)
    diagonal = iota((k, k * points), 0) == iota((k, k * points), 1) // points
    lefts = []
    for b in range(blocks):
        moving = one_hot(iota((points, points), 0) == partner[b:b + 1])
        there = jnp.dot(parts, moving, preferred_element_type=F32)
        rows = []
        for c in range(3):
            r = 3 * c * blocks + b
            found = there[r:r + 1] + there[r + blocks:r + blocks + 1]
            found = found + there[r + 2 * blocks:r + 2 * blocks + 1]
            row = stiffness_ref[b] * (found - points_ref[c, b:b + 1, :])
            rows.append(jnp.where(diagonal, jnp.concatenate([row] * k, axis=1), 0.0))
        rows.append(jnp.zeros_like(rows[0]))
        lefts.append(jnp.concatenate(rows, axis=0).astype(BF16))

    owner_row = to_row(owners_ref[:, 0, :])
    places = slot_row(owner_row, to_column(owner_row), devices)
    total = devices * per_owner
    chosen = iota((total, places.shape[1]), 0) == places
    selector = one_hot(chosen)

    for b in range(blocks):
        wait_block(b)
        right = loaded_ref[b].reshape(k * points, patch)
        result = jnp.dot(lefts[b], right, preferred_element_type=F32)
        for c in range(3):
            contrib_ref[c, b * k:(b + 1) * k, :] = result[c * k:(c + 1) * k]

    tiles = patch // LANES
    width = 3 * tiles * per_owner
    for c in range(3):
        packed = jnp.dot(selector, contrib_ref[c].astype(BF16), preferred_element_type=F32)
        for p in range(per_owner):
            for t in range(tiles):
                stage_ref[pl.ds(p * 3 * tiles + c * tiles + t, devices, stride=width), :] = (
                    packed[p * devices:(p + 1) * devices, t * LANES:(t + 1) * LANES]
                )
    out_ref[...] = stage_ref[...].reshape(out_ref.shape).astype(BF16)
    column = jnp.max(jnp.where(chosen, to_row(slots_ref[...]), -1), axis=1, keepdims=True)
    lane = iota((devices, LANES), 1)
    table = jnp.full((devices, LANES), -1, I32)
    for p in range(per_owner):
        table = jnp.where(lane == p, column[p * devices:(p + 1) * devices], table)
    for d in range(devices):
        table_ref[d] = table[d:d + 1]


HBM = pl.BlockSpec(memory_space=pltpu.HBM)


def each_peer(rows_grid, columns_grid, visit, carry=0):
    gx, gy = lax.axis_index("gx"), lax.axis_index("gy")
    ys = [lax.rem(gy + dy, columns_grid) for dy in range(columns_grid)]
    for dy in range(1, columns_grid):
        visit(dy, (gx, ys[dy]))

    def row(dx, carry):
        x = lax.rem(gx + dx, rows_grid)
        for dy in range(columns_grid):
            visit(dx * columns_grid + dy, (x, ys[dy]))
        return carry

    lax.fori_loop(1, rows_grid, row, 0)


def start_swap(rows_grid, columns_grid, source, target, send_sem, recv_sem):
    devices = rows_grid * columns_grid
    me = lax.axis_index("gx") * columns_grid + lax.axis_index("gy")

    def start(off, to):
        pltpu.make_async_remote_copy(
            src_ref=source.at[to[0] * columns_grid + to[1]], dst_ref=target.at[me],
            send_sem=send_sem, recv_sem=recv_sem, device_id=to, device_id_type=MESH,
        ).start()

    each_peer(rows_grid, columns_grid, start)
    pltpu.make_async_copy(source.at[me], target.at[me], recv_sem).start()

    def wait():
        sent = pl.ds(0, devices - 1)
        pltpu.make_async_copy(source, target, recv_sem).wait()
        pltpu.make_async_copy(source.at[sent], target.at[sent], send_sem).wait()

    return wait


def unpack(stage_ref, devices, per_owner, tiles, c):
    width = 3 * tiles * per_owner
    rows = []
    for p in range(per_owner):
        rows.append(jnp.concatenate(
            [stage_ref[pl.ds(p * 3 * tiles + c * tiles + t, devices, stride=width), :]
             for t in range(tiles)], axis=1))
    return jnp.concatenate(rows, axis=0)


def table_row(table_ref, devices, per_owner):
    total = devices * per_owner
    row = jnp.zeros((1, total), I32)
    for p in range(per_owner):
        column = table_ref[:, 0, :][:, p:p + 1]
        spot = iota((devices, total), 1) == p * devices + iota((devices, total), 0)
        row = row + jnp.sum(jnp.where(spot, column, 0), axis=0, keepdims=True)
    return row


def table_column(table_ref, per_owner):
    return jnp.concatenate([table_ref[:, 0, :][:, p:p + 1] for p in range(per_owner)], axis=0)


def one_hot(mask):
    return mask.astype(F32).astype(BF16)


PAD = 8
UNROLL = 4
assert viscosity == transport_rate
keep = 1.0 - 6.0 * viscosity


def sweep(mid, east, west, north, south, above, below):
    coefficients = [(1 - m, 1 + m) for m in mid]
    out = []
    for c in range(3):
        pairs = [
            ahead * front[c] + behind * back[c]
            for (ahead, behind), (front, back) in zip(
                coefficients, ((east, west), (north, south), (above, below)))
        ]
        out.append(pairs[0] + (pairs[1] + pairs[2]))
    return out


def step_kernel(
    rows_grid, columns_grid, per_owner, points_in, stiffness_in, links_in, owners_in,
    slots_in, weights_ref, velocity_ref,
    fluid_ref, loaded_ref, returned_ref, partial_ref,
    points_ref, stiffness_ref, links_ref, owners_ref, slots_ref, small_sem, received_ref, table_ref, out_ref, outtable_ref, replies_ref, contrib_ref, stage_ref,
    force_ref, first_ref, second_ref, first_half, second_half, placing_ref, taking_ref, sides_send, sides_recv, ends_send, ends_recv,
    halo_ref, send_sem, recv_sem, load_sem, block_sem,
    hsend_sem, hrecv_sem,
):
    devices = rows_grid * columns_grid
    total = devices * per_owner
    tiles, _, layers, rows, _ = fluid_ref.shape
    blocks = weights_ref.shape[0]
    groups = rows // 8
    order = [*range(1, groups - 1), groups - 1, 0]
    pairs = [tuple(order[n:n + 2]) for n in range(0, groups, 2)]
    stride = first_ref.shape[3]
    flat_shape = (3, tiles, layers * stride, LANES)

    def block(b):
        return pltpu.make_async_copy(weights_ref.at[b], loaded_ref.at[b], block_sem.at[b])

    def load(t):
        return pltpu.make_async_copy(
            velocity_ref.at[:, :, :, pl.ds(t * LANES, LANES)], fluid_ref.at[t], load_sem.at[t])

    small = [
        pltpu.make_async_copy(source, target, small_sem.at[n])
        for n, (source, target) in enumerate((
            (points_in, points_ref), (stiffness_in, stiffness_ref), (links_in, links_ref),
            (owners_in, owners_ref), (slots_in, slots_ref)))
    ]
    for copy in small:
        copy.start()
    for b in range(blocks):
        block(b).start(priority=1)

    def wait_block(b):
        block(b).wait()
        if b == blocks - 1:
            for t in range(tiles):
                load(t).start()

    gx, gy = lax.axis_index("gx"), lax.axis_index("gy")
    barrier = pltpu.get_barrier_semaphore()

    def hello(off, to):
        pl.semaphore_signal(barrier, inc=1, device_id=to, device_id_type=MESH)

    each_peer(rows_grid, columns_grid, hello)
    for copy in small:
        copy.wait()
    spread(
        devices, per_owner, points_ref, stiffness_ref, links_ref, owners_ref, slots_ref,
        loaded_ref, out_ref, outtable_ref, contrib_ref, stage_ref, wait_block)
    pl.semaphore_wait(barrier, devices - 1)
    wait_table = start_swap(
        rows_grid, columns_grid, outtable_ref, table_ref, send_sem.at[0], recv_sem.at[0])
    wait = start_swap(
        rows_grid, columns_grid, out_ref, received_ref, send_sem.at[1], recv_sem.at[1])
    for t in range(tiles):
        load(t).wait()
    wait_table()
    chunk = 8
    cells = chunk * rows
    slots_row = table_row(table_ref, devices, per_owner)
    placing_ref[...] = one_hot(iota((layers * rows, total), 0) == slots_row)
    slots = table_column(table_ref, per_owner)
    taking_ref[...] = one_hot(iota((total, layers * rows), 1) == slots)
    wait()

    stage_ref[...] = received_ref[...].astype(F32).reshape(stage_ref.shape)
    for c in range(3):
        force = (force_step * unpack(stage_ref, devices, per_owner, tiles, c)).astype(BF16)
        for n, t in enumerate((0, tiles - 1, *range(1, tiles - 1))):
            force_ref[c, :, n * LANES:(n + 1) * LANES] = force[:, t * LANES:(t + 1) * LANES]
    lane = iota((16, LANES), 1)
    at_first, at_last = lane == 0, lane == LANES - 1

    unit = one_hot(at_first | at_last)

    def edge_lane(z, k):
        return 2 * (z * len(pairs) + k) + 1

    def gather_end(j, mark, low, high, total_so_far):
        return total_so_far + mark * pltpu.roll(jnp.where(at_first, low, high), j, 1)

    zero = jnp.zeros((16, LANES), BF16)

    def settle(first, wanted, n, ends):
        ends = list(ends)
        placing = placing_ref[pl.ds(pl.multiple_of(n * cells, cells), cells), :]
        marks = {
            (k, n_pair): pltpu.roll(unit, edge_lane(n * chunk + k, n_pair), 1)
            for k in range(chunk) for n_pair in range(len(pairs)) if ends
        }
        for c in range(3):
            push = jnp.dot(
                placing, force_ref[c, :, first * LANES:(first + len(wanted)) * LANES],
                preferred_element_type=F32)
            for k in range(chunk):
                z = n * chunk + k
                edges = {}
                for m, t in enumerate(wanted):
                    value = fluid_ref[t, c, z] + push[
                        k * rows:(k + 1) * rows, m * LANES:(m + 1) * LANES]
                    first_ref[c, t, z, PAD:PAD + rows, :] = value
                    for n_pair, pair in enumerate(pairs):
                        packed = jnp.concatenate(
                            [value[8 * g:8 * g + 8] for g in pair], axis=0).astype(BF16)
                        first_half[c, t, z, 16 * n_pair:16 * n_pair + 16, :] = packed
                        edges[t, n_pair] = packed
                for n_pair in range(len(pairs) if ends else 0):
                    ends[c] = gather_end(
                        edge_lane(z, n_pair), marks[k, n_pair], edges[0, n_pair],
                        edges[tiles - 1, n_pair], ends[c])
        return tuple(ends)

    has = [gx > 0, gx < rows_grid - 1, gy > 0, gy < columns_grid - 1]

    def copies_of(step, wanted=range(4)):
        plan = [
            (sides_send.at[step, 0], sides_recv.at[step, 1], (-1, 0), has[0], has[1]),
            (sides_send.at[step, 1], sides_recv.at[step, 0], (1, 0), has[1], has[0]),
            (ends_send.at[step], ends_recv.at[step, 1], (0, -1), has[2], has[3]),
            (ends_send.at[step], ends_recv.at[step, 0], (0, 1), has[3], has[2]),
        ]
        out = []
        for n, (source, target, (dx, dy), sends, receives) in enumerate(plan):
            if n not in wanted:
                continue
            to = (lax.rem(gx + dx + rows_grid, rows_grid),
                  lax.rem(gy + dy + columns_grid, columns_grid))
            out.append((pltpu.make_async_remote_copy(
                src_ref=source, dst_ref=target, send_sem=hsend_sem.at[step, n],
                recv_sem=hrecv_sem.at[step, n], device_id=to, device_id_type=MESH),
                sends, receives))
        return out

    def send(step, wanted):
        for copy, sends, _ in copies_of(step, wanted):
            @pl.when(sends)
            def _():
                copy.start()

    def send_sides(step, ref):
        flat = ref.reshape(flat_shape)
        for side in range(2):
            row = PAD + side * (rows - 1)
            for c in range(3):
                for t in range(tiles):
                    sides_send[step, side, c, t] = jnp.concatenate(
                        [flat[c, t, pl.ds(g * stride + row, 8, stride=stride), :]
                         for g in range(0, layers, 8)], axis=0).astype(BF16)
        send(step, (0, 1))

    def send_ends(step, ends):
        for c in range(3):
            ends_send[step, c] = ends[c]
        send(step, (2, 3))

    def wait_ends(step):
        for copy, _, receives in copies_of(step, (2, 3)):
            @pl.when(receives)
            def _():
                copy.wait_recv()
        even = lax.rem(lane, 2) == 0
        for c in range(3):
            south, north = [ends_recv[step, side, c].astype(F32) for side in range(2)]
            halo_ref[c] = jnp.where(
                even, jnp.where(has[2], south, 0.0), jnp.where(has[3], north, 0.0)).astype(BF16)

    def wait_sides(step, ref):
        flat = ref.reshape(flat_shape)
        for copy, _, receives in copies_of(step, (0, 1)):
            @pl.when(receives)
            def _():
                copy.wait_recv()
        for side in range(2):
            row = PAD - 1 if side == 0 else PAD + rows
            for c in range(3):
                for t in range(tiles):
                    value = jnp.where(has[side], sides_recv[step, side, c, t].astype(F32), 0.0)
                    for g in range(0, layers, 8):
                        flat[c, t, pl.ds(g * stride + row, 8, stride=stride), :] = value[g:g + 8]

    def sweep_tiles(ref, half, z, k, wanted):
        up, down = lax.rem(z + 1, layers), lax.rem(z + layers - 1, layers)
        j = edge_lane(z, k)
        at = slice(16 * k, 16 * k + 16)

        def beside(c, t, offset):
            return jnp.concatenate(
                [ref[c, t, z, PAD + 8 * g + offset:PAD + 8 * g + offset + 8, :]
                 for g in pairs[k]], axis=0)

        whole, mids = {}, {}

        def mid(c, t):
            if (c, t) not in mids:
                whole[c, t] = beside(c, t, 0)
                mids[c, t] = whole[c, t].astype(BF16)
            return mids[c, t]

        outside = {}

        def beyond(c):
            if c not in outside:
                outside[c] = pltpu.roll(halo_ref[c], LANES - j, 1)
            return outside[c]

        def north(c, t):
            if t == tiles - 1:
                after = beyond(c)
            else:
                after = mid(c, t + 1)
            return pltpu.roll(jnp.where(at_first, after, mid(c, t)), LANES - 1, 1)

        def south(c, t):
            if t == 0:
                before = beyond(c)
            else:
                before = mid(c, t - 1)
            return pltpu.roll(jnp.where(at_last, before, mid(c, t)), 1, 1)

        for t in wanted:
            parts = []
            for c in range(3):
                parts.append((
                    mid(c, t), beside(c, t, 1).astype(BF16), beside(c, t, -1).astype(BF16),
                    north(c, t), south(c, t),
                    half[c, t, up, at, :], half[c, t, down, at, :]))
            change = sweep(*[list(v) for v in zip(*parts)])
            yield t, [keep * whole[c, t] + transport_rate * change[c].astype(F32)
                      for c in range(3)]

    def run(ref, half, store, groups_wanted, tiles_wanted, ends=()):
        edge = len(ends) > 0
        unroll = max(1, min(layers, 4 * UNROLL // (len(groups_wanted) * len(tiles_wanted))))

        def body(i, ends):
            ends = list(ends)
            for m in range(unroll):
                z = i * unroll + m
                for k in groups_wanted:
                    edges = {}
                    for t, new in sweep_tiles(ref, half, z, k, tiles_wanted):
                        for c in range(3):
                            edges[c, t] = store(c, t, z, k, new[c])
                    if edge:
                        j = edge_lane(z, k)
                        mark = pltpu.roll(unit, j, 1)
                        for c in range(3):
                            ends[c] = gather_end(
                                j, mark, edges[c, 0], edges[c, tiles - 1], ends[c])
            return tuple(ends)

        return lax.fori_loop(0, layers // unroll, body, ends)

    inner, outer = tuple(range(len(pairs) - 1)), (len(pairs) - 1,)
    middle, border = tuple(range(1, tiles - 1)), (0, tiles - 1)
    half_tiles = tiles // 2
    ends = lax.fori_loop(
        0, layers // chunk, functools.partial(settle, 0, border), (zero,) * 3)
    send_ends(0, ends)
    lax.fori_loop(0, layers // chunk, functools.partial(settle, len(border), middle), ())
    send_sides(0, first_ref)
    def store_first(c, t, z, k, value):
        for m, g in enumerate(pairs[k]):
            second_ref[c, t, z, PAD + 8 * g:PAD + 8 * g + 8, :] = value[8 * m:8 * m + 8]
        packed = value.astype(BF16)
        second_half[c, t, z, 16 * k:16 * k + 16, :] = packed
        return packed

    step_one = functools.partial(run, first_ref, first_half, store_first)
    step_one(inner, middle)
    wait_ends(0)
    ends = step_one(inner, border, (zero,) * 3)
    wait_sides(0, first_ref)
    ends = step_one(outer, border, ends)
    send_ends(1, ends)
    step_one(outer, middle)
    send_sides(1, second_ref)

    def store_second(c, t, z, k, value):
        for m, g in enumerate(pairs[k]):
            fluid_ref[t, c, z, 8 * g:8 * g + 8, :] = value[8 * m:8 * m + 8]

    step_two = functools.partial(run, second_ref, second_half, store_second)
    wide = replies_ref.shape[2]
    waits = []
    step_two(inner, middle)
    wait_ends(1)
    step_two(inner, border)
    wait_sides(1, second_ref)
    for h in range(2):
        mine = tuple(range(h * half_tiles, (h + 1) * half_tiles))
        step_two(outer, mine)
        for c in range(3):
            flat = jnp.concatenate(
                [fluid_ref[t, c].reshape(layers * rows, LANES).astype(BF16) for t in mine], axis=1)
            part = jnp.dot(taking_ref[...], flat, preferred_element_type=F32)
            for p in range(per_owner):
                for n in range(half_tiles):
                    row = (p * 3 + c) * half_tiles + n
                    stage_ref[pl.ds(row, devices, stride=wide), :] = (
                        part[p * devices:(p + 1) * devices, n * LANES:(n + 1) * LANES])
        replies_ref[h] = stage_ref[0:devices * wide, :].reshape(replies_ref.shape[1:]).astype(BF16)
        waits.append(start_swap(
            rows_grid, columns_grid, replies_ref.at[h], returned_ref.at[h],
            send_sem.at[2 + h], recv_sem.at[2 + h]))
    for step in range(STEPS):
        for copy, sends, _ in copies_of(step):
            @pl.when(sends)
            def _():
                copy.wait_send()
    owner_row = to_row(owners_ref[:, 0, :])
    places = slot_column(owner_row, to_column(owner_row), devices)
    selector = one_hot(iota((places.shape[0], total), 1) == places)
    waits[0]()

    def emit(c, b, value):
        partial_ref[c, b:b + 1, :] = value

    interpolate(0, devices, per_owner, returned_ref, loaded_ref, selector, stage_ref, emit)
    waits[1]()


def interpolate(h, devices, per_owner, returned_ref, loaded_ref, selector, stage_ref, emit):
    blocks, k, points, patch = loaded_ref.shape
    half_tiles = patch // LANES // 2
    wide = returned_ref.shape[2]
    stage_ref[0:devices * wide, :] = returned_ref[h].astype(F32).reshape(devices * wide, LANES)
    picked = []
    for c in range(3):
        replies = jnp.concatenate(
            [jnp.concatenate(
                [stage_ref[pl.ds((p * 3 + c) * half_tiles + n, devices, stride=wide), :]
                 for n in range(half_tiles)], axis=1)
             for p in range(per_owner)], axis=0).astype(BF16)
        picked.append(jnp.dot(selector, replies, preferred_element_type=F32))
    diagonal = iota((k, k * points), 0) == iota((k, k * points), 1) // points
    span = half_tiles * LANES
    for b in range(blocks):
        rows = [picked[c][b * k:(b + 1) * k, :] for c in range(3)]
        rows.append(jnp.zeros_like(rows[0]))
        left = jnp.concatenate(rows, axis=0).astype(BF16)
        right = loaded_ref[b, :, :, h * span:(h + 1) * span].reshape(k * points, span)
        result = lax.dot_general(
            left, right, (((1,), (1,)), ((), ())), preferred_element_type=F32)
        for c in range(3):
            own = jnp.where(diagonal, result[c * k:(c + 1) * k], 0.0)
            fold = own[:, 0:points]
            for n in range(1, k):
                fold = fold + own[:, n * points:(n + 1) * points]
            emit(c, b, jnp.sum(fold, axis=0, keepdims=True))


def finish_kernel(
    devices, per_owner, fluid_ref, loaded_ref, returned_ref, partial_ref, owners_in, points_in,
    out_ref, moved_ref, owners_ref, points_ref, stage_ref, small_sem, store_sem,
):
    def store(t):
        return pltpu.make_async_copy(
            fluid_ref.at[t], out_ref.at[:, :, :, pl.ds(t * LANES, LANES)], store_sem.at[t])

    small = [
        pltpu.make_async_copy(owners_in, owners_ref, small_sem.at[0]),
        pltpu.make_async_copy(points_in, points_ref, small_sem.at[1]),
    ]
    for copy in small:
        copy.start()
    for t in range(fluid_ref.shape[0]):
        store(t).start()
    for copy in small:
        copy.wait()
    owner_row = to_row(owners_ref[:, 0, :])
    places = slot_column(owner_row, to_column(owner_row), devices)
    selector = one_hot(iota((places.shape[0], devices * per_owner), 1) == places)

    def emit(c, b, value):
        moved_ref[c, b:b + 1, :] = points_ref[c, b:b + 1, :] + fiber_step * (
            partial_ref[c, b:b + 1, :] + value)

    interpolate(1, devices, per_owner, returned_ref, loaded_ref, selector, stage_ref, emit)
    for t in range(fluid_ref.shape[0]):
        store(t).wait()


def shards(rows_grid, columns_grid, velocity, fiber_points, stiffness, links, delta_weights,
           owners, patch_slots):
    blocks, intersection, points, patch = delta_weights.shape
    _, layers, rows, columns = velocity.shape
    devices = rows_grid * columns_grid
    entries = blocks * intersection
    per_owner = max(2, (2 * entries + devices - 1) // devices)
    total = devices * per_owner
    tiles = patch // LANES
    width = 3 * tiles * per_owner
    owners = jnp.transpose(owners, (0, 2, 1))
    points_first = jnp.transpose(fiber_points, (1, 0, 2))
    message = jax.ShapeDtypeStruct((devices, width, LANES), BF16)
    wide = -(-3 * (tiles // 2) * per_owner // 8) * 8
    reply = jax.ShapeDtypeStruct((2, devices, wide, LANES), BF16)
    table_shape = jax.ShapeDtypeStruct((devices, 1, LANES), I32)
    stage = pltpu.VMEM((devices * max(width, wide), LANES), F32)
    limit = 36 << 20
    field = pltpu.VMEM((3, tiles, layers, rows + 2 * PAD, LANES), F32)
    half = pltpu.VMEM((3, tiles, layers, rows, LANES), BF16)
    sides = pltpu.VMEM((STEPS, 2, 3, tiles, layers, LANES), BF16)
    fluid_tiles, weights, returned, partial = pl.pallas_call(
        functools.partial(step_kernel, rows_grid, columns_grid, per_owner),
        out_shape=[
            jax.ShapeDtypeStruct((tiles, 3, layers, rows, LANES), F32),
            jax.ShapeDtypeStruct(delta_weights.shape, BF16),
            reply,
            jax.ShapeDtypeStruct(points_first.shape, F32),
        ],
        in_specs=[HBM] * 7,
        out_specs=[VMEM] * 4,
        scratch_shapes=[
            pltpu.VMEM(points_first.shape, F32),
            pltpu.SMEM(stiffness.shape, F32),
            pltpu.VMEM(links.shape, I32),
            pltpu.VMEM(owners.shape, I32),
            pltpu.VMEM(patch_slots.shape, I32),
            pltpu.SemaphoreType.DMA((5,)),
            pltpu.VMEM(message.shape, BF16),
            pltpu.VMEM(table_shape.shape, I32),
            pltpu.VMEM(message.shape, BF16),
            pltpu.VMEM(table_shape.shape, I32),
            pltpu.VMEM(reply.shape, BF16),
            pltpu.VMEM((3, entries, patch), F32),
            stage,
            pltpu.VMEM((3, total, patch), BF16),
            field, field, half, half,
            pltpu.VMEM((layers * rows, total), BF16),
            pltpu.VMEM((total, layers * rows), BF16),
            sides, sides,
            pltpu.VMEM((STEPS, 3, 16, LANES), BF16),
            pltpu.VMEM((STEPS, 2, 3, 16, LANES), BF16),
            pltpu.VMEM((3, 16, LANES), BF16),
            pltpu.SemaphoreType.DMA((4,)),
            pltpu.SemaphoreType.DMA((4,)),
            pltpu.SemaphoreType.DMA((tiles,)),
            pltpu.SemaphoreType.DMA((blocks,)),
            pltpu.SemaphoreType.DMA((STEPS, 4)),
            pltpu.SemaphoreType.DMA((STEPS, 4)),
        ],
        compiler_params=pltpu.CompilerParams(
            collective_id=0, has_side_effects=True, vmem_limit_bytes=limit),
    )(*[pltpu.with_memory_space_constraint(v, pltpu.HBM) for v in (
        points_first, stiffness, links, owners, patch_slots, delta_weights, velocity)])

    fluid, moved = pl.pallas_call(
        functools.partial(finish_kernel, devices, per_owner),
        out_shape=[
            jax.ShapeDtypeStruct(velocity.shape, F32),
            jax.ShapeDtypeStruct(points_first.shape, F32),
        ],
        in_specs=[VMEM, VMEM, VMEM, VMEM, HBM, HBM],
        out_specs=[HBM, VMEM],
        scratch_shapes=[
            pltpu.VMEM(owners.shape, I32),
            pltpu.VMEM(points_first.shape, F32),
            stage,
            pltpu.SemaphoreType.DMA((2,)),
            pltpu.SemaphoreType.DMA((tiles,)),
        ],
        compiler_params=pltpu.CompilerParams(vmem_limit_bytes=8 << 20),
    )(fluid_tiles, weights, returned, partial, pltpu.with_memory_space_constraint(owners, pltpu.HBM),
      pltpu.with_memory_space_constraint(points_first, pltpu.HBM))
    return fluid, jnp.transpose(moved, (1, 0, 2))


def solution(mesh):
    placed = (
        P(None, None, "gx", "gy"),
        P(("gx", "gy"), None, None),
        P(("gx", "gy")),
        P(("gx", "gy"), None),
        P(("gx", "gy"), None, None, None),
        P(("gx", "gy"), None, None),
        P(("gx", "gy"), None),
    )
    return jax.shard_map(
        functools.partial(shards, mesh.shape["gx"], mesh.shape["gy"]),
        mesh=mesh,
        in_specs=placed,
        out_specs=(placed[0], placed[1]),
        check_vma=False,
    )
```

```python
import functools

import jax
import jax.numpy as jnp
from jax import lax
from jax.experimental import pallas as pl
from jax.experimental.pallas import tpu as pltpu
from jax.sharding import PartitionSpec as P

STEPS = 2
viscosity = 0.1
transport_rate = 0.1
force_step = 0.5
fiber_step = 0.25

F32 = jnp.float32
BF16 = jnp.bfloat16
I32 = jnp.int32
LANES = 128
MESH = pl.DeviceIdType.MESH
VMEM = pl.BlockSpec(memory_space=pltpu.VMEM)
ANY = pl.BlockSpec(memory_space=pl.ANY)
SMEM = pl.BlockSpec(memory_space=pltpu.SMEM)


def iota(shape, dim):
    return lax.broadcasted_iota(I32, shape, dim)


def to_column(row):
    n = row.shape[1]
    return jnp.sum(jnp.where(iota((n, n), 0) == iota((n, n), 1), row, 0), axis=1, keepdims=True)


def to_row(grid):
    n, k = grid.shape
    tiled = jnp.concatenate([grid] * n, axis=1)
    return jnp.sum(
        jnp.where(iota((n, n * k), 0) == iota((n, n * k), 1) // k, tiled, 0), axis=0, keepdims=True)


def slot_row(owner_row, owner_column, devices):
    n = owner_row.shape[1]
    same = (owner_column == owner_row) & (iota((n, n), 0) < iota((n, n), 1))
    rank = jnp.sum(jnp.where(same, 1, 0), axis=0, keepdims=True)
    return rank * devices + owner_row


def slot_column(owner_row, owner_column, devices):
    n = owner_row.shape[1]
    same = (owner_column == owner_row) & (iota((n, n), 1) < iota((n, n), 0))
    rank = jnp.sum(jnp.where(same, 1, 0), axis=1, keepdims=True)
    return rank * devices + owner_column


def spread(
    devices, per_owner, points_ref, stiffness_ref, links_ref, owners_ref, slots_ref, loaded_ref,
    out_ref, table_ref, contrib_ref, stage_ref, wait_block,
):
    blocks, k, points, patch = loaded_ref.shape
    parts = []
    for c in range(3):
        rest = points_ref[c]
        for _ in range(3):
            part = rest.astype(BF16).astype(F32)
            parts.append(part)
            rest = rest - part
    parts.append(jnp.zeros_like(parts[0]))
    parts = jnp.concatenate(parts, axis=0).astype(BF16)
    partner = lax.rem(iota(links_ref.shape, 1) + links_ref[...], points)
    diagonal = iota((k, k * points), 0) == iota((k, k * points), 1) // points
    lefts = []
    for b in range(blocks):
        moving = one_hot(iota((points, points), 0) == partner[b:b + 1])
        there = jnp.dot(parts, moving, preferred_element_type=F32)
        rows = []
        for c in range(3):
            r = 3 * c * blocks + b
            found = there[r:r + 1] + there[r + blocks:r + blocks + 1]
            found = found + there[r + 2 * blocks:r + 2 * blocks + 1]
            row = stiffness_ref[b] * (found - points_ref[c, b:b + 1, :])
            rows.append(jnp.where(diagonal, jnp.concatenate([row] * k, axis=1), 0.0))
        rows.append(jnp.zeros_like(rows[0]))
        lefts.append(jnp.concatenate(rows, axis=0).astype(BF16))

    owner_row = to_row(owners_ref[:, 0, :])
    places = slot_row(owner_row, to_column(owner_row), devices)
    total = devices * per_owner
    chosen = iota((total, places.shape[1]), 0) == places
    selector = one_hot(chosen)

    for b in range(blocks):
        wait_block(b)
        right = loaded_ref[b].reshape(k * points, patch)
        result = jnp.dot(lefts[b], right, preferred_element_type=F32)
        for c in range(3):
            contrib_ref[c, b * k:(b + 1) * k, :] = result[c * k:(c + 1) * k]

    tiles = patch // LANES
    width = 3 * tiles * per_owner
    for c in range(3):
        packed = jnp.dot(selector, contrib_ref[c].astype(BF16), preferred_element_type=F32)
        for p in range(per_owner):
            for t in range(tiles):
                stage_ref[pl.ds(p * 3 * tiles + c * tiles + t, devices, stride=width), :] = (
                    packed[p * devices:(p + 1) * devices, t * LANES:(t + 1) * LANES]
                )
    out_ref[...] = stage_ref[...].reshape(out_ref.shape).astype(BF16)
    column = jnp.max(jnp.where(chosen, to_row(slots_ref[...]), -1), axis=1, keepdims=True)
    lane = iota((devices, LANES), 1)
    table = jnp.full((devices, LANES), -1, I32)
    for p in range(per_owner):
        table = jnp.where(lane == p, column[p * devices:(p + 1) * devices], table)
    for d in range(devices):
        table_ref[d] = table[d:d + 1]


HBM = pl.BlockSpec(memory_space=pltpu.HBM)


def each_peer(rows_grid, columns_grid, visit, carry=0):
    gx, gy = lax.axis_index("gx"), lax.axis_index("gy")
    ys = [lax.rem(gy + dy, columns_grid) for dy in range(columns_grid)]
    for dy in range(1, columns_grid):
        visit(dy, (gx, ys[dy]))

    def row(dx, carry):
        x = lax.rem(gx + dx, rows_grid)
        for dy in range(columns_grid):
            visit(dx * columns_grid + dy, (x, ys[dy]))
        return carry

    lax.fori_loop(1, rows_grid, row, 0)


def start_swap(rows_grid, columns_grid, source, target, send_sem, recv_sem):
    devices = rows_grid * columns_grid
    me = lax.axis_index("gx") * columns_grid + lax.axis_index("gy")

    def start(off, to):
        pltpu.make_async_remote_copy(
            src_ref=source.at[to[0] * columns_grid + to[1]], dst_ref=target.at[me],
            send_sem=send_sem, recv_sem=recv_sem, device_id=to, device_id_type=MESH,
        ).start()

    each_peer(rows_grid, columns_grid, start)
    pltpu.make_async_copy(source.at[me], target.at[me], recv_sem).start()

    def wait():
        sent = pl.ds(0, devices - 1)
        pltpu.make_async_copy(source, target, recv_sem).wait()
        pltpu.make_async_copy(source.at[sent], target.at[sent], send_sem).wait()

    return wait


def unpack(stage_ref, devices, per_owner, tiles, c):
    width = 3 * tiles * per_owner
    rows = []
    for p in range(per_owner):
        rows.append(jnp.concatenate(
            [stage_ref[pl.ds(p * 3 * tiles + c * tiles + t, devices, stride=width), :]
             for t in range(tiles)], axis=1))
    return jnp.concatenate(rows, axis=0)


def table_row(table_ref, devices, per_owner):
    total = devices * per_owner
    row = jnp.zeros((1, total), I32)
    for p in range(per_owner):
        column = table_ref[:, 0, :][:, p:p + 1]
        spot = iota((devices, total), 1) == p * devices + iota((devices, total), 0)
        row = row + jnp.sum(jnp.where(spot, column, 0), axis=0, keepdims=True)
    return row


def table_column(table_ref, per_owner):
    return jnp.concatenate([table_ref[:, 0, :][:, p:p + 1] for p in range(per_owner)], axis=0)


def one_hot(mask):
    return mask.astype(F32).astype(BF16)


PAD = 8
UNROLL = 4
assert viscosity == transport_rate
keep = 1.0 - 6.0 * viscosity


def sweep(mid, east, west, north, south, above, below):
    coefficients = [(1 - m, 1 + m) for m in mid]
    out = []
    for c in range(3):
        pairs = [
            ahead * front[c] + behind * back[c]
            for (ahead, behind), (front, back) in zip(
                coefficients, ((east, west), (north, south), (above, below)))
        ]
        out.append(pairs[0] + (pairs[1] + pairs[2]))
    return out


def step_kernel(
    rows_grid, columns_grid, per_owner, points_in, stiffness_in, links_in, owners_in,
    slots_in, weights_ref, velocity_ref,
    fluid_ref, loaded_ref, returned_ref, partial_ref,
    points_ref, stiffness_ref, links_ref, owners_ref, slots_ref, small_sem, received_ref, table_ref, out_ref, outtable_ref, replies_ref, contrib_ref, stage_ref,
    force_ref, first_ref, second_ref, first_half, second_half, placing_ref, taking_ref, sides_send, sides_recv, ends_send, ends_recv,
    halo_ref, send_sem, recv_sem, load_sem, block_sem,
    hsend_sem, hrecv_sem,
):
    devices = rows_grid * columns_grid
    total = devices * per_owner
    tiles, _, layers, rows, _ = fluid_ref.shape
    blocks = weights_ref.shape[0]
    groups = rows // 8
    order = [*range(1, groups - 1), groups - 1, 0]
    pairs = [tuple(order[n:n + 2]) for n in range(0, groups, 2)]
    stride = first_ref.shape[3]
    flat_shape = (3, tiles, layers * stride, LANES)

    def block(b):
        return pltpu.make_async_copy(weights_ref.at[b], loaded_ref.at[b], block_sem.at[b])

    def load(t):
        return pltpu.make_async_copy(
            velocity_ref.at[:, :, :, pl.ds(t * LANES, LANES)], fluid_ref.at[t], load_sem.at[t])

    small = [
        pltpu.make_async_copy(source, target, small_sem.at[n])
        for n, (source, target) in enumerate((
            (points_in, points_ref), (stiffness_in, stiffness_ref), (links_in, links_ref),
            (owners_in, owners_ref), (slots_in, slots_ref)))
    ]
    for copy in small:
        copy.start()
    for b in range(blocks):
        block(b).start(priority=1)

    def wait_block(b):
        block(b).wait()
        if b == blocks - 1:
            for t in range(tiles):
                load(t).start()

    gx, gy = lax.axis_index("gx"), lax.axis_index("gy")
    barrier = pltpu.get_barrier_semaphore()

    def hello(off, to):
        pl.semaphore_signal(barrier, inc=1, device_id=to, device_id_type=MESH)

    each_peer(rows_grid, columns_grid, hello)
    for copy in small:
        copy.wait()
    spread(
        devices, per_owner, points_ref, stiffness_ref, links_ref, owners_ref, slots_ref,
        loaded_ref, out_ref, outtable_ref, contrib_ref, stage_ref, wait_block)
    pl.semaphore_wait(barrier, devices - 1)
    wait_table = start_swap(
        rows_grid, columns_grid, outtable_ref, table_ref, send_sem.at[0], recv_sem.at[0])
    wait = start_swap(
        rows_grid, columns_grid, out_ref, received_ref, send_sem.at[1], recv_sem.at[1])
    for t in range(tiles):
        load(t).wait()
    wait_table()
    chunk = 8
    cells = chunk * rows
    slots_row = table_row(table_ref, devices, per_owner)
    placing_ref[...] = one_hot(iota((layers * rows, total), 0) == slots_row)
    slots = table_column(table_ref, per_owner)
    taking_ref[...] = one_hot(iota((total, layers * rows), 1) == slots)
    wait()

    stage_ref[...] = received_ref[...].astype(F32).reshape(stage_ref.shape)
    for c in range(3):
        force = (force_step * unpack(stage_ref, devices, per_owner, tiles, c)).astype(BF16)
        for n, t in enumerate((0, tiles - 1, *range(1, tiles - 1))):
            force_ref[c, :, n * LANES:(n + 1) * LANES] = force[:, t * LANES:(t + 1) * LANES]
    lane = iota((16, LANES), 1)
    at_first, at_last = lane == 0, lane == LANES - 1

    unit = one_hot(at_first | at_last)

    def edge_lane(z, k):
        return 2 * (z * len(pairs) + k) + 1

    def gather_end(j, mark, low, high, total_so_far):
        return total_so_far + mark * pltpu.roll(jnp.where(at_first, low, high), j, 1)

    zero = jnp.zeros((16, LANES), BF16)

    def settle(first, wanted, n, ends):
        ends = list(ends)
        placing = placing_ref[pl.ds(pl.multiple_of(n * cells, cells), cells), :]
        marks = {
            (k, n_pair): pltpu.roll(unit, edge_lane(n * chunk + k, n_pair), 1)
            for k in range(chunk) for n_pair in range(len(pairs)) if ends
        }
        for c in range(3):
            push = jnp.dot(
                placing, force_ref[c, :, first * LANES:(first + len(wanted)) * LANES],
                preferred_element_type=F32)
            for k in range(chunk):
                z = n * chunk + k
                edges = {}
                for m, t in enumerate(wanted):
                    value = fluid_ref[t, c, z] + push[
                        k * rows:(k + 1) * rows, m * LANES:(m + 1) * LANES]
                    first_ref[c, t, z, PAD:PAD + rows, :] = value
                    for n_pair, pair in enumerate(pairs):
                        packed = jnp.concatenate(
                            [value[8 * g:8 * g + 8] for g in pair], axis=0).astype(BF16)
                        first_half[c, t, z, 16 * n_pair:16 * n_pair + 16, :] = packed
                        edges[t, n_pair] = packed
                for n_pair in range(len(pairs) if ends else 0):
                    ends[c] = gather_end(
                        edge_lane(z, n_pair), marks[k, n_pair], edges[0, n_pair],
                        edges[tiles - 1, n_pair], ends[c])
        return tuple(ends)

    has = [gx > 0, gx < rows_grid - 1, gy > 0, gy < columns_grid - 1]

    def copies_of(step, wanted=range(6)):
        plan = [
            *[(sides_send.at[step, part, 0], sides_recv.at[step, part, 1], (-1, 0), has[0], has[1])
              for part in range(2)],
            *[(sides_send.at[step, part, 1], sides_recv.at[step, part, 0], (1, 0), has[1], has[0])
              for part in range(2)],
            (ends_send.at[step], ends_recv.at[step, 1], (0, -1), has[2], has[3]),
            (ends_send.at[step], ends_recv.at[step, 0], (0, 1), has[3], has[2]),
        ]
        out = []
        for n, (source, target, (dx, dy), sends, receives) in enumerate(plan):
            if n not in wanted:
                continue
            to = (lax.rem(gx + dx + rows_grid, rows_grid),
                  lax.rem(gy + dy + columns_grid, columns_grid))
            out.append((pltpu.make_async_remote_copy(
                src_ref=source, dst_ref=target, send_sem=hsend_sem.at[step, n],
                recv_sem=hrecv_sem.at[step, n], device_id=to, device_id_type=MESH),
                sends, receives))
        return out

    def send(step, wanted):
        for copy, sends, _ in copies_of(step, wanted):
            @pl.when(sends)
            def _():
                copy.start()

    def send_sides(step, ref, part):
        flat = ref.reshape(flat_shape)
        for side in range(2):
            row = PAD + side * (rows - 1)
            for c in range(3):
                for n, t in enumerate((border, middle)[part]):
                    sides_send[step, part, side, c, n] = jnp.concatenate(
                        [flat[c, t, pl.ds(g * stride + row, 8, stride=stride), :]
                         for g in range(0, layers, 8)], axis=0).astype(BF16)
        send(step, (part, 2 + part))

    def send_ends(step, ends):
        for c in range(3):
            ends_send[step, c] = ends[c]
        send(step, (4, 5))

    def wait_ends(step):
        for copy, _, receives in copies_of(step, (4, 5)):
            @pl.when(receives)
            def _():
                copy.wait_recv()
        even = lax.rem(lane, 2) == 0
        for c in range(3):
            south, north = [ends_recv[step, side, c].astype(F32) for side in range(2)]
            halo_ref[c] = jnp.where(
                even, jnp.where(has[2], south, 0.0), jnp.where(has[3], north, 0.0)).astype(BF16)

    def wait_sides(step, ref):
        flat = ref.reshape(flat_shape)
        for copy, _, receives in copies_of(step, range(4)):
            @pl.when(receives)
            def _():
                copy.wait_recv()
        for side in range(2):
            row = PAD - 1 if side == 0 else PAD + rows
            for part in range(2):
                for c in range(3):
                    for n, t in enumerate((border, middle)[part]):
                        value = jnp.where(
                            has[side], sides_recv[step, part, side, c, n].astype(F32), 0.0)
                        for g in range(0, layers, 8):
                            flat[c, t, pl.ds(g * stride + row, 8, stride=stride), :] = (
                                value[g:g + 8])

    def sweep_tiles(ref, half, z, k, wanted):
        up, down = lax.rem(z + 1, layers), lax.rem(z + layers - 1, layers)
        j = edge_lane(z, k)
        at = slice(16 * k, 16 * k + 16)

        def beside(c, t, offset):
            return jnp.concatenate(
                [ref[c, t, z, PAD + 8 * g + offset:PAD + 8 * g + offset + 8, :]
                 for g in pairs[k]], axis=0)

        whole, mids = {}, {}

        def mid(c, t):
            if (c, t) not in mids:
                whole[c, t] = beside(c, t, 0)
                mids[c, t] = whole[c, t].astype(BF16)
            return mids[c, t]

        outside = {}

        def beyond(c):
            if c not in outside:
                outside[c] = pltpu.roll(halo_ref[c], LANES - j, 1)
            return outside[c]

        def north(c, t):
            if t == tiles - 1:
                after = beyond(c)
            else:
                after = mid(c, t + 1)
            return pltpu.roll(jnp.where(at_first, after, mid(c, t)), LANES - 1, 1)

        def south(c, t):
            if t == 0:
                before = beyond(c)
            else:
                before = mid(c, t - 1)
            return pltpu.roll(jnp.where(at_last, before, mid(c, t)), 1, 1)

        for t in wanted:
            parts = []
            for c in range(3):
                parts.append((
                    mid(c, t), beside(c, t, 1).astype(BF16), beside(c, t, -1).astype(BF16),
                    north(c, t), south(c, t),
                    half[c, t, up, at, :], half[c, t, down, at, :]))
            change = sweep(*[list(v) for v in zip(*parts)])
            yield t, [keep * whole[c, t] + transport_rate * change[c].astype(F32)
                      for c in range(3)]

    def run(ref, half, store, groups_wanted, tiles_wanted, ends=()):
        edge = len(ends) > 0
        unroll = max(1, min(layers, 4 * UNROLL // (len(groups_wanted) * len(tiles_wanted))))

        def body(i, ends):
            ends = list(ends)
            for m in range(unroll):
                z = i * unroll + m
                for k in groups_wanted:
                    edges = {}
                    for t, new in sweep_tiles(ref, half, z, k, tiles_wanted):
                        for c in range(3):
                            edges[c, t] = store(c, t, z, k, new[c])
                    if edge:
                        j = edge_lane(z, k)
                        mark = pltpu.roll(unit, j, 1)
                        for c in range(3):
                            ends[c] = gather_end(
                                j, mark, edges[c, 0], edges[c, tiles - 1], ends[c])
            return tuple(ends)

        return lax.fori_loop(0, layers // unroll, body, ends)

    inner, outer = tuple(range(len(pairs) - 1)), (len(pairs) - 1,)
    middle, border = tuple(range(1, tiles - 1)), (0, tiles - 1)
    half_tiles = tiles // 2
    ends = lax.fori_loop(
        0, layers // chunk, functools.partial(settle, 0, border), (zero,) * 3)
    send_ends(0, ends)
    send_sides(0, first_ref, 0)
    lax.fori_loop(0, layers // chunk, functools.partial(settle, len(border), middle), ())
    send_sides(0, first_ref, 1)
    def store_first(c, t, z, k, value):
        for m, g in enumerate(pairs[k]):
            second_ref[c, t, z, PAD + 8 * g:PAD + 8 * g + 8, :] = value[8 * m:8 * m + 8]
        packed = value.astype(BF16)
        second_half[c, t, z, 16 * k:16 * k + 16, :] = packed
        return packed

    step_one = functools.partial(run, first_ref, first_half, store_first)
    step_one(inner, middle)
    wait_ends(0)
    ends = step_one(inner, border, (zero,) * 3)
    wait_sides(0, first_ref)
    ends = step_one(outer, border, ends)
    send_ends(1, ends)
    send_sides(1, second_ref, 0)
    step_one(outer, middle)
    send_sides(1, second_ref, 1)

    def store_second(c, t, z, k, value):
        for m, g in enumerate(pairs[k]):
            fluid_ref[t, c, z, 8 * g:8 * g + 8, :] = value[8 * m:8 * m + 8]

    step_two = functools.partial(run, second_ref, second_half, store_second)
    wide = replies_ref.shape[2]
    waits = []
    step_two(inner, middle)
    wait_ends(1)
    step_two(inner, border)
    wait_sides(1, second_ref)
    for h in range(2):
        mine = tuple(range(h * half_tiles, (h + 1) * half_tiles))
        step_two(outer, mine)
        for c in range(3):
            flat = jnp.concatenate(
                [fluid_ref[t, c].reshape(layers * rows, LANES).astype(BF16) for t in mine], axis=1)
            part = jnp.dot(taking_ref[...], flat, preferred_element_type=F32)
            for p in range(per_owner):
                for n in range(half_tiles):
                    row = (p * 3 + c) * half_tiles + n
                    stage_ref[pl.ds(row, devices, stride=wide), :] = (
                        part[p * devices:(p + 1) * devices, n * LANES:(n + 1) * LANES])
        replies_ref[h] = stage_ref[0:devices * wide, :].reshape(replies_ref.shape[1:]).astype(BF16)
        waits.append(start_swap(
            rows_grid, columns_grid, replies_ref.at[h], returned_ref.at[h],
            send_sem.at[2 + h], recv_sem.at[2 + h]))
    for step in range(STEPS):
        for copy, sends, _ in copies_of(step):
            @pl.when(sends)
            def _():
                copy.wait_send()
    owner_row = to_row(owners_ref[:, 0, :])
    places = slot_column(owner_row, to_column(owner_row), devices)
    selector = one_hot(iota((places.shape[0], total), 1) == places)
    waits[0]()

    def emit(c, b, value):
        partial_ref[c, b:b + 1, :] = value

    interpolate(0, devices, per_owner, returned_ref, loaded_ref, selector, stage_ref, emit)
    waits[1]()


def interpolate(h, devices, per_owner, returned_ref, loaded_ref, selector, stage_ref, emit):
    blocks, k, points, patch = loaded_ref.shape
    half_tiles = patch // LANES // 2
    wide = returned_ref.shape[2]
    stage_ref[0:devices * wide, :] = returned_ref[h].astype(F32).reshape(devices * wide, LANES)
    picked = []
    for c in range(3):
        replies = jnp.concatenate(
            [jnp.concatenate(
                [stage_ref[pl.ds((p * 3 + c) * half_tiles + n, devices, stride=wide), :]
                 for n in range(half_tiles)], axis=1)
             for p in range(per_owner)], axis=0).astype(BF16)
        picked.append(jnp.dot(selector, replies, preferred_element_type=F32))
    diagonal = iota((k, k * points), 0) == iota((k, k * points), 1) // points
    span = half_tiles * LANES
    for b in range(blocks):
        rows = [picked[c][b * k:(b + 1) * k, :] for c in range(3)]
        rows.append(jnp.zeros_like(rows[0]))
        left = jnp.concatenate(rows, axis=0).astype(BF16)
        right = loaded_ref[b, :, :, h * span:(h + 1) * span].reshape(k * points, span)
        result = lax.dot_general(
            left, right, (((1,), (1,)), ((), ())), preferred_element_type=F32)
        for c in range(3):
            own = jnp.where(diagonal, result[c * k:(c + 1) * k], 0.0)
            fold = own[:, 0:points]
            for n in range(1, k):
                fold = fold + own[:, n * points:(n + 1) * points]
            emit(c, b, jnp.sum(fold, axis=0, keepdims=True))


def finish_kernel(
    devices, per_owner, fluid_ref, loaded_ref, returned_ref, partial_ref, owners_in, points_in,
    out_ref, moved_ref, owners_ref, points_ref, stage_ref, small_sem, store_sem,
):
    def store(t):
        return pltpu.make_async_copy(
            fluid_ref.at[t], out_ref.at[:, :, :, pl.ds(t * LANES, LANES)], store_sem.at[t])

    small = [
        pltpu.make_async_copy(owners_in, owners_ref, small_sem.at[0]),
        pltpu.make_async_copy(points_in, points_ref, small_sem.at[1]),
    ]
    for copy in small:
        copy.start()
    for t in range(fluid_ref.shape[0]):
        store(t).start()
    for copy in small:
        copy.wait()
    owner_row = to_row(owners_ref[:, 0, :])
    places = slot_column(owner_row, to_column(owner_row), devices)
    selector = one_hot(iota((places.shape[0], devices * per_owner), 1) == places)

    def emit(c, b, value):
        moved_ref[c, b:b + 1, :] = points_ref[c, b:b + 1, :] + fiber_step * (
            partial_ref[c, b:b + 1, :] + value)

    interpolate(1, devices, per_owner, returned_ref, loaded_ref, selector, stage_ref, emit)
    for t in range(fluid_ref.shape[0]):
        store(t).wait()


def shards(rows_grid, columns_grid, velocity, fiber_points, stiffness, links, delta_weights,
           owners, patch_slots):
    blocks, intersection, points, patch = delta_weights.shape
    _, layers, rows, columns = velocity.shape
    devices = rows_grid * columns_grid
    entries = blocks * intersection
    per_owner = max(2, (2 * entries + devices - 1) // devices)
    total = devices * per_owner
    tiles = patch // LANES
    width = 3 * tiles * per_owner
    owners = jnp.transpose(owners, (0, 2, 1))
    points_first = jnp.transpose(fiber_points, (1, 0, 2))
    message = jax.ShapeDtypeStruct((devices, width, LANES), BF16)
    wide = -(-3 * (tiles // 2) * per_owner // 8) * 8
    reply = jax.ShapeDtypeStruct((2, devices, wide, LANES), BF16)
    table_shape = jax.ShapeDtypeStruct((devices, 1, LANES), I32)
    stage = pltpu.VMEM((devices * max(width, wide), LANES), F32)
    limit = 36 << 20
    field = pltpu.VMEM((3, tiles, layers, rows + 2 * PAD, LANES), F32)
    half = pltpu.VMEM((3, tiles, layers, rows, LANES), BF16)
    sides = pltpu.VMEM((STEPS, 2, 2, 3, tiles // 2, layers, LANES), BF16)
    fluid_tiles, weights, returned, partial = pl.pallas_call(
        functools.partial(step_kernel, rows_grid, columns_grid, per_owner),
        out_shape=[
            jax.ShapeDtypeStruct((tiles, 3, layers, rows, LANES), F32),
            jax.ShapeDtypeStruct(delta_weights.shape, BF16),
            reply,
            jax.ShapeDtypeStruct(points_first.shape, F32),
        ],
        in_specs=[HBM] * 7,
        out_specs=[VMEM] * 4,
        scratch_shapes=[
            pltpu.VMEM(points_first.shape, F32),
            pltpu.SMEM(stiffness.shape, F32),
            pltpu.VMEM(links.shape, I32),
            pltpu.VMEM(owners.shape, I32),
            pltpu.VMEM(patch_slots.shape, I32),
            pltpu.SemaphoreType.DMA((5,)),
            pltpu.VMEM(message.shape, BF16),
            pltpu.VMEM(table_shape.shape, I32),
            pltpu.VMEM(message.shape, BF16),
            pltpu.VMEM(table_shape.shape, I32),
            pltpu.VMEM(reply.shape, BF16),
            pltpu.VMEM((3, entries, patch), F32),
            stage,
            pltpu.VMEM((3, total, patch), BF16),
            field, field, half, half,
            pltpu.VMEM((layers * rows, total), BF16),
            pltpu.VMEM((total, layers * rows), BF16),
            sides, sides,
            pltpu.VMEM((STEPS, 3, 16, LANES), BF16),
            pltpu.VMEM((STEPS, 2, 3, 16, LANES), BF16),
            pltpu.VMEM((3, 16, LANES), BF16),
            pltpu.SemaphoreType.DMA((4,)),
            pltpu.SemaphoreType.DMA((4,)),
            pltpu.SemaphoreType.DMA((tiles,)),
            pltpu.SemaphoreType.DMA((blocks,)),
            pltpu.SemaphoreType.DMA((STEPS, 6)),
            pltpu.SemaphoreType.DMA((STEPS, 6)),
        ],
        compiler_params=pltpu.CompilerParams(
            collective_id=0, has_side_effects=True, vmem_limit_bytes=limit),
    )(*[pltpu.with_memory_space_constraint(v, pltpu.HBM) for v in (
        points_first, stiffness, links, owners, patch_slots, delta_weights, velocity)])

    fluid, moved = pl.pallas_call(
        functools.partial(finish_kernel, devices, per_owner),
        out_shape=[
            jax.ShapeDtypeStruct(velocity.shape, F32),
            jax.ShapeDtypeStruct(points_first.shape, F32),
        ],
        in_specs=[VMEM, VMEM, VMEM, VMEM, HBM, HBM],
        out_specs=[HBM, VMEM],
        scratch_shapes=[
            pltpu.VMEM(owners.shape, I32),
            pltpu.VMEM(points_first.shape, F32),
            stage,
            pltpu.SemaphoreType.DMA((2,)),
            pltpu.SemaphoreType.DMA((tiles,)),
        ],
        compiler_params=pltpu.CompilerParams(vmem_limit_bytes=8 << 20),
    )(fluid_tiles, weights, returned, partial, pltpu.with_memory_space_constraint(owners, pltpu.HBM),
      pltpu.with_memory_space_constraint(points_first, pltpu.HBM))
    return fluid, jnp.transpose(moved, (1, 0, 2))


def solution(mesh):
    placed = (
        P(None, None, "gx", "gy"),
        P(("gx", "gy"), None, None),
        P(("gx", "gy")),
        P(("gx", "gy"), None),
        P(("gx", "gy"), None, None, None),
        P(("gx", "gy"), None, None),
        P(("gx", "gy"), None),
    )
    return jax.shard_map(
        functools.partial(shards, mesh.shape["gx"], mesh.shape["gy"]),
        mesh=mesh,
        in_specs=placed,
        out_specs=(placed[0], placed[1]),
        check_vma=False,
    )
```
